256 devices in a mesh: dir: 16 (over x_hi, y, core), psi: 16 (over z, x_lo).
Axes of the slice: x: 4 (x_hi: 2, x_lo: 2; x = x_hi * 2 + x_lo), y: 4, z: 8, core: 2. Of those that a mesh axis runs over, the one named last changes fastest.
Arguments:
- images: float32 [32768, 9216], P(('dir', 'psi')), may hold values from -6 to 6
- prior_bin: int32 [32768], P(('dir', 'psi')), may hold values from 0 to 63, as said below
- prior_center: int32 [32768], P(('dir', 'psi')), may hold values from 0 to 63, as said below
- defocus_class: int32 [32768], P(('dir', 'psi')), may hold values from 0 to 15
- templates: float32 [64, 64, 9216], P('dir', 'psi'), may hold values from -0.125 to 0.125
- ctf_table: float32 [16, 9216], replicated, may hold values from -1 to 1
Outputs:
- log_total: float32 [32768], P(('dir', 'psi'))
- mean_shift: float32 [32768], P(('dir', 'psi'))
- average: float32 [64, 64, 9216], P('dir', 'psi')
The draws below stay inside these ranges and needn't reach their ends.
Inputs may be any that keep to these rules, and one draw needn't show every extreme that they name: `prior_bin`: in each aligned block of 128 rows (the particles of one device) no bin is named more than 4 times, and some bin exactly 4 times. `prior_center`: A particle in aligned block q of 128 rows has its prior centre among the 4 angles that start at (q mod 16) * 4.
All inputs are finite; a program needn't handle non-finite values.
Results may differ from the reference program's by a relative error of at most 0.0003.
Values sent between devices are 32-bit elements; how exact they have to be, the bound alone decides.
No kernel may reach another device: no remote copies, remote signals or barrier semaphores. Data moves between devices by JAX's collectives and lax.ppermute only.
A program may use at most 128 MiB of HBM per device.

```python
import math
import jax
import jax.numpy as jnp
from jax import lax

PIX = 9216
NCLS = 16
HALF = 4
CAP_BIN = 4
ANG_DEV = 4
PART_DEV = 128
BINS = 64
ANGLES = 64
PARTICLES = 32768
N_DIR = 16
N_PSI = 16


def draw_prior_bin(key, part):
    blocks = N_DIR * N_PSI
    slots = BINS * CAP_BIN
    key_heavy, key_full, key_noise = jax.random.split(key, 3)
    heavy = jax.random.randint(key_heavy, (blocks, BINS), 0, 3)
    full_bin = jax.random.randint(key_full, (blocks,), 0, BINS)
    heavy = jnp.where(jnp.arange(BINS)[None, :] == full_bin[:, None], 64, heavy)
    noise = jax.random.randint(key_noise, (blocks, slots), 0, 1024)
    slot_bin = jnp.arange(slots) // CAP_BIN
    ranking = (noise + jnp.take(heavy, slot_bin, axis=1) * 512) * slots + jnp.arange(slots)[None, :]
    picked_scores, chosen = lax.top_k(ranking, PART_DEV)
    return (chosen // CAP_BIN).reshape(-1).astype(jnp.int32)


def draw_prior_center(key, part):
    rows = N_DIR * N_PSI * PART_DEV
    column = jnp.arange(rows) // PART_DEV % N_PSI
    return (column * ANG_DEV + jax.random.randint(key, (rows,), 0, ANG_DEV)).astype(jnp.int32)


def set_ends(entries, own_key, least, top_value):
    longest = entries.shape.index(max(entries.shape))
    spots = []
    for shift in (0, 1):
        where = [jax.random.randint(jax.random.fold_in(own_key, axis), (), 0, length) for axis, length in enumerate(entries.shape)]
        where[longest] = (where[longest] + shift) % entries.shape[longest]
        spots.append(tuple(where))
    return entries.at[spots[0]].set(least).at[spots[1]].set(top_value)


def steps_of(stream_key, extent, cuts, low, top_value):
    def one(dim, shards_of):
        heights = jax.random.uniform(jax.random.fold_in(jax.random.fold_in(stream_key, 6), dim), (shards_of,), jnp.float32, low / len(cuts), top_value / len(cuts))
        return jnp.repeat(jnp.exp(heights), extent[dim] // shards_of).reshape((-1,) + (1,) * (len(extent) - dim - 1))

    factor_of = one(*cuts[0])
    for cut in cuts[1:]:
        factor_of = factor_of * one(*cut)
    return factor_of


def gaussian(key, dims, spread, most, cuts=(), held_as=jnp.bfloat16):
    result = spread * jax.random.normal(key, dims, jnp.float32)
    if cuts:
        result = result * steps_of(key, dims, cuts, -0.22, 0.18)
    return jnp.clip(result, -most, most).astype(held_as)


def setup_inputs(seed: int = 0) -> dict:
    streams_of = jax.random.split(jax.random.key(seed), 7)
    images = gaussian(streams_of[0], (PARTICLES, PIX), 1.0, 6.0, ((0, 256),), jnp.float32)
    prior_bin = draw_prior_bin(jax.random.fold_in(streams_of[6], 71), 0)
    prior_center = draw_prior_center(jax.random.fold_in(streams_of[6], 71), 0)
    defocus_class = set_ends(jax.random.randint(streams_of[3], (PARTICLES,), 0, NCLS), jax.random.fold_in(streams_of[3], 1), 0, NCLS - 1).astype(jnp.int32)
    templates = gaussian(streams_of[4], (BINS, ANGLES, PIX), (PIX // 4) ** -0.5, 0.125, ((0, 16), (1, 16)), jnp.float32)
    ctf_table = jnp.clip(jax.random.uniform(streams_of[5], (NCLS, PIX), jnp.float32, -1.0, 1.0), -1.0, 1.0)
    return dict(images=images, prior_bin=prior_bin, prior_center=prior_center, defocus_class=defocus_class, templates=templates, ctf_table=ctf_table)


def reference(images, prior_bin, prior_center, defocus_class, templates, ctf_table):
    highest = lax.Precision.HIGHEST
    block_rows = math.gcd(PARTICLES, 512)
    blocks = PARTICLES // block_rows
    offsets = jnp.arange(-HALF, HALF + 1, dtype=jnp.int32)
    shift_values = offsets.astype(jnp.float32)
    flat_templates = templates.reshape(BINS * ANGLES, PIX)

    def score_block(carry, portion):
        data_sum, weight_sum = carry
        image_rows, bin_rows, centre_rows, class_rows = portion
        ctf_rows = ctf_table[class_rows]
        weighted = ctf_rows * image_rows
        angle_ids = ((centre_rows[:, None] + offsets[None, :]) % ANGLES).astype(jnp.int32)
        flat_index = (bin_rows[:, None] * ANGLES + angle_ids).astype(jnp.int32)
        picked = flat_templates[flat_index]
        crossed = jnp.einsum("nk,nok->no", weighted, picked, precision=highest)
        quadratic = jnp.einsum("nk,nok->no", ctf_rows * ctf_rows, picked * picked, precision=highest)
        scores = crossed - 0.5 * quadratic
        log_total = jnp.log(jnp.sum(jnp.exp(scores), axis=1))
        posterior = jnp.exp(scores - log_total[:, None])
        mean_shift = jnp.sum(posterior * shift_values[None, :], axis=1)
        flat_rows = flat_index.reshape(-1)
        data_sum = data_sum.at[flat_rows].add((posterior[:, :, None] * weighted[:, None, :]).reshape(-1, PIX))
        weight_sum = weight_sum.at[flat_rows].add((posterior[:, :, None] * (ctf_rows * ctf_rows)[:, None, :]).reshape(-1, PIX))
        return (data_sum, weight_sum), (log_total, mean_shift)

    start_sums = jnp.zeros((BINS * ANGLES, PIX), jnp.float32)
    portions = (images.reshape(blocks, block_rows, PIX), prior_bin.reshape(blocks, block_rows),
                prior_center.reshape(blocks, block_rows), defocus_class.reshape(blocks, block_rows))
    (data_sum, weight_sum), (log_total, mean_shift) = lax.scan(score_block, (start_sums, start_sums), portions)
    average = (data_sum / (weight_sum + 1.0)).reshape(BINS, ANGLES, PIX)
    return log_total.reshape(-1), mean_shift.reshape(-1), average
```

```python
import jax
import jax.numpy as jnp
from jax import lax
from jax.experimental import pallas as pl
from jax.experimental.pallas import tpu as pltpu
from jax.sharding import Mesh
from jax.sharding import PartitionSpec as P

HALF = 4
LANES = 128
CLASSES = 16
IMG = 288
TPL = 40
ROWS = IMG + TPL
META = 36
BF = jnp.bfloat16
F32 = jnp.float32
HIGHEST = lax.Precision.HIGHEST
PLANE = ("dir", "xlo")


def params(mib):
    return pltpu.CompilerParams(vmem_limit_bytes=mib * 1024 * 1024)


def cost(flops, moved):
    return pl.CostEstimate(flops=flops, bytes_accessed=moved, transcendentals=0)


def lane_group(shape):
    return lax.broadcasted_iota(jnp.int32, shape, len(shape) - 1) // 32


def turned(x, groups):
    groups = groups % 4
    return x if groups == 0 else pltpu.roll(x, 32 * groups, x.ndim - 1)


def pick_groups(parts):
    group = lane_group(parts[0].shape)
    out = parts[3]
    for q in (2, 1, 0):
        out = jnp.where(group == q, parts[q], out)
    return out


def split(x):
    hi = x.astype(BF)
    return hi, (x - hi.astype(F32)).astype(BF)


def pack_kernel(img_ref, rem_ref, tpl_ref, tplrem_ref, meta_ref, out_ref):
    meta = meta_ref[...]
    for q in range(4):
        for j in range(2):
            tile = pl.ds((2 * q + j) * LANES, LANES)
            out_ref[q, pl.ds(j * 128, 128), :] = img_ref[:, tile]
            for b in range(4):
                out_ref[q, pl.ds(IMG + 16 * j + 4 * b, 4), :] = tpl_ref[b, :, tile]
        out_ref[q, pl.ds(256, 32), :] = pick_groups([turned(rem_ref[pl.ds(32 * g, 32), :], g - q) for g in range(4)])
        out_ref[q, pl.ds(IMG + 32, 4), :] = pick_groups([turned(tplrem_ref[b], b - q) for b in range(4)])
        out_ref[q, pl.ds(IMG + META, 4), :] = meta


def pack(images, templates, meta):
    steps = 8
    return pl.pallas_call(
        pack_kernel,
        grid=(steps,),
        in_specs=[
            pl.BlockSpec((128, 1024), lambda t: (0, t)),
            pl.BlockSpec((128, LANES), lambda t: (0, 64 + t)),
            pl.BlockSpec((4, 4, 1024), lambda t: (0, 0, t)),
            pl.BlockSpec((4, 4, LANES), lambda t: (0, 0, 64 + t)),
            pl.BlockSpec((4, LANES), lambda t: (0, 0)),
        ],
        out_specs=pl.BlockSpec((4, ROWS, LANES), lambda t: (t, 0, 0)),
        out_shape=jax.ShapeDtypeStruct((4 * steps, ROWS, LANES), F32),
        compiler_params=params(16),
        cost_estimate=cost(0, 11_000_000),
        name="pack",
    )(images, images, templates, templates, meta)


def fill_templates(tpl_ref, sources, sq_ref, tf_ref, base, yh_ref, yl_ref, yr_ref):
    for d, s in enumerate(sources):
        rows = pl.ds(16 * d, 16)
        tf_ref[rows, pl.ds(0, 128)] = tpl_ref[s, pl.ds(0, 16), :]
        tf_ref[rows, pl.ds(128, 128)] = tpl_ref[s, pl.ds(16, 16), :]
        packed = tpl_ref[s, pl.ds(32, 4), :]
        v = [turned(packed, j) for j in range(4)]
        for b in range(4):
            tf_ref[pl.ds(16 * d + 4 * b, 4), pl.ds(256, 128)] = pick_groups([v[(q - b) % 4] for q in (0, 1, 2)] + [jnp.zeros_like(packed)])
    for c in range(4):
        rows = pl.ds(64 * c, 64)
        out = pl.ds(base + 64 * c, 64)
        full = tf_ref[rows, :]
        quad = jnp.dot(full * full, sq_ref[...], precision=HIGHEST, preferred_element_type=F32)
        hi, lo = split(full)
        yh_ref[out, :] = hi[:, :256]
        yl_ref[out, :] = lo[:, :256]
        vh, vl = split(-0.5 * quad)
        lane = lax.broadcasted_iota(jnp.int32, (64, LANES), 1)
        last = jnp.where(lane < 112, vh.astype(F32), vl.astype(F32))
        tail = jnp.where(lane < 64, hi[:, 256:].astype(F32), lo[:, 256:].astype(F32))
        yr_ref[out, :] = jnp.where(lane < 96, tail, last).astype(BF)


def gathered(yh_ref, yl_ref, yr_ref, rows, x):
    y = jnp.concatenate([yh_ref[rows, :], yl_ref[rows, :], yh_ref[rows, :], yr_ref[rows, :]], axis=1)
    return lax.dot_general(y, x, (((1,), (1,)), ((), ())), preferred_element_type=F32)


def by_bin(scores, first_bin, bins):
    rows = scores.shape[0]
    row_bin = lax.broadcasted_iota(jnp.int32, scores.shape, 0) // 4 + first_bin
    kept = jnp.where(row_bin == bins, scores, 0.0)
    return jnp.sum(kept.reshape(rows // 8, 8, scores.shape[1]), axis=0)


def bins_of(tpl_ref, first, second):
    both = [tpl_ref[s, pl.ds(META, 1), :] for s in (first, second)]
    return jnp.concatenate(both, axis=1).astype(jnp.int32)


def window(yh_ref, yl_ref, yr_ref, base, x, bins):
    total = jnp.zeros((8, 256), F32)
    for c in range(2):
        part = gathered(yh_ref, yl_ref, yr_ref, pl.ds(base + 128 * c, 128), x)
        total = total + by_bin(part, 32 * c, bins)
    return total + pltpu.roll(total, 4, 0)


def own_kernel(buf_ref, tpl_ref, ctf_ref, sq_ref, xh_ref, xl_ref, xr_ref, out_ref, tf_ref, yh_ref, yl_ref, yr_ref, ce_ref):
    step = pl.program_id(0)

    @pl.when(step == 0)
    def _():
        for side in range(2):
            fill_templates(tpl_ref, [2 * d + side for d in range(16)], sq_ref, tf_ref, 256 * side, yh_ref, yl_ref, yr_ref)
        ctf = ctf_ref[...]
        hi, mid = split(ctf)
        low = (ctf - hi.astype(F32) - mid.astype(F32)).astype(BF)
        ce_ref[pl.ds(0, 16), :] = hi
        ce_ref[pl.ds(16, 16), :] = mid
        ce_ref[pl.ds(32, 16), :] = low

    half = lax.broadcasted_iota(jnp.int32, (8, 128), 0) < 4
    group = lane_group((128, LANES))
    for s in range(4):
        source = 4 * step + s
        classes = tpl_ref[source, pl.ds(META + 2, 1), :].astype(jnp.int32)
        row_class = lax.broadcasted_iota(jnp.int32, (48, 128), 0) % CLASSES
        onehot = jnp.where(row_class == classes, 1.0, 0.0).astype(BF)
        ctf = lax.dot_general(onehot, ce_ref[...], (((0,), (0,)), ((), ())), preferred_element_type=F32)
        for j in range(2):
            hi, lo = split(ctf[:, 128 * j : 128 * j + 128] * buf_ref[s, pl.ds(128 * j, 128), :])
            xh_ref[s, :, pl.ds(128 * j, 128)] = hi
            xl_ref[s, :, pl.ds(128 * j, 128)] = lo
        packed = buf_ref[s, pl.ds(256, 32), :]
        v = [turned(packed, j) for j in range(4)]
        one = jnp.ones_like(packed)
        rem = jnp.concatenate([pick_groups([v[(q - g) % 4] for q in (0, 1, 2)] + [one]) for g in range(4)], axis=0)
        hi, lo = split(ctf[:, 256:] * rem)
        xr_ref[s, :, :] = jnp.where(group == 1, lo.astype(F32), hi.astype(F32)).astype(BF)
    for side in range(2):
        first, second = side, 2 + side
        x = jnp.concatenate(
            [jnp.concatenate([xh_ref[s], xh_ref[s], xl_ref[s], xr_ref[s]], axis=1) for s in (first, second)], axis=0
        )
        bins = bins_of(tpl_ref, 4 * step + first, 4 * step + second)
        low = window(yh_ref, yl_ref, yr_ref, 0, x, bins)
        high = window(yh_ref, yl_ref, yr_ref, 256, x, bins)
        for k, s in enumerate((first, second)):
            cols = slice(128 * k, 128 * k + 128)
            out_ref[s] = jnp.where(half, low[:, cols], high[:, cols])


def own_scores(buf, tpl, ctf_ext, squares):
    n = buf.shape[0]
    whole = lambda shape: pl.BlockSpec(shape, lambda p: (0,) * len(shape))
    block = lambda *shape: pl.BlockSpec(shape, lambda p: (p,) + (0,) * (len(shape) - 1))
    return pl.pallas_call(
        own_kernel,
        grid=(n // 4,),
        in_specs=[block(4, IMG, LANES), whole((n, TPL, LANES)), whole((16, 384)), whole((384, LANES))],
        out_specs=[block(4, 128, 256), block(4, 128, 256), block(4, 128, 128), block(4, 8, 128)],
        out_shape=[
            jax.ShapeDtypeStruct((n, 128, 256), BF),
            jax.ShapeDtypeStruct((n, 128, 256), BF),
            jax.ShapeDtypeStruct((n, 128, 128), BF),
            jax.ShapeDtypeStruct((n, 8, 128), F32),
        ],
        scratch_shapes=[
            pltpu.VMEM((256, 384), F32),
            pltpu.VMEM((512, 256), BF),
            pltpu.VMEM((512, 256), BF),
            pltpu.VMEM((512, 128), BF),
            pltpu.VMEM((48, 384), BF),
        ],
        compiler_params=params(24),
        cost_estimate=cost(4_000_000_000, 12_000_000),
        name="own_scores",
    )(buf, tpl, ctf_ext, squares)


def halo_kernel(xh_ref, xl_ref, xr_ref, own_ref, tpl_ref, halo_ref, sq_ref, out_ref, tf_ref, yh_ref, yl_ref, yr_ref):
    step = pl.program_id(0)

    @pl.when(step == 0)
    def _():
        for side in range(2):
            fill_templates(halo_ref, [16 * side + d for d in range(16)], sq_ref, tf_ref, 256 * side, yh_ref, yl_ref, yr_ref)

    for side in range(2):
        first, second = side, 2 + side
        x = jnp.concatenate(
            [jnp.concatenate([xh_ref[s], xh_ref[s], xl_ref[s], xr_ref[s]], axis=1) for s in (first, second)], axis=0
        )
        bins = bins_of(tpl_ref, 4 * step + first, 4 * step + second)
        edge = window(yh_ref, yl_ref, yr_ref, 256 * side, x, bins)
        for k, s in enumerate((first, second)):
            out_ref[s, pl.ds(0, 8), :] = own_ref[s]
            out_ref[s, pl.ds(8, 8), :] = edge[:, 128 * k : 128 * k + 128]


def halo_scores(xh, xl, xr, own, tpl, halo, squares):
    n = xh.shape[0]
    whole = lambda shape: pl.BlockSpec(shape, lambda p: (0,) * len(shape))
    block = lambda *shape: pl.BlockSpec(shape, lambda p: (p,) + (0,) * (len(shape) - 1))
    return pl.pallas_call(
        halo_kernel,
        grid=(n // 4,),
        in_specs=[
            block(4, 128, 256),
            block(4, 128, 256),
            block(4, 128, 128),
            block(4, 8, 128),
            whole((n, TPL, LANES)),
            whole((n, TPL, LANES)),
            whole((384, LANES)),
        ],
        out_specs=block(4, 16, 128),
        out_shape=jax.ShapeDtypeStruct((n, 16, 128), F32),
        scratch_shapes=[
            pltpu.VMEM((256, 384), F32),
            pltpu.VMEM((512, 256), BF),
            pltpu.VMEM((512, 256), BF),
            pltpu.VMEM((512, 128), BF),
        ],
        compiler_params=params(24),
        cost_estimate=cost(2_000_000_000, 6_000_000),
        name="halo_scores",
    )(xh, xl, xr, own, tpl, halo, squares)


def home_kernel(place_ref, scores_ref, centre_ref, total_ref, shift_ref, p_ref):
    xlo = place_ref[0]
    first = place_ref[1]
    n = scores_ref.shape[0]
    scores = scores_ref[0]
    for s in range(1, n):
        scores = scores + scores_ref[s]
    row = lax.broadcasted_iota(jnp.int32, scores.shape, 0)
    angle = jnp.where(row < 8, row + 4, row - 8 + 12 * xlo)
    offset = angle - (centre_ref[...] - first + 4)
    inside = jnp.logical_and(jnp.abs(offset) <= HALF, row < 12)
    safe = jnp.where(inside, scores, 0.0)
    total = jnp.log(jnp.sum(jnp.where(inside, jnp.exp(safe), 0.0), axis=0, keepdims=True))
    p = jnp.where(inside, jnp.exp(safe - total), 0.0)
    total_ref[...] = total
    shift_ref[...] = jnp.sum(p * offset.astype(F32), axis=0, keepdims=True)
    p = jnp.where(row < 12, p, pltpu.roll(p, 4, 0))
    for s in range(n):
        p_ref[s] = p


def home(place, scores, centre):
    n = scores.shape[0]
    vmem = pl.BlockSpec(memory_space=pltpu.VMEM)
    return pl.pallas_call(
        home_kernel,
        in_specs=[pl.BlockSpec(memory_space=pltpu.SMEM), vmem, vmem],
        out_specs=[vmem, vmem, vmem],
        out_shape=[
            jax.ShapeDtypeStruct((1, 128), F32),
            jax.ShapeDtypeStruct((1, 128), F32),
            jax.ShapeDtypeStruct((n, 16, 128), F32),
        ],
        compiler_params=params(4),
        cost_estimate=cost(200_000, 600_000),
        name="home",
    )(place, scores, centre)


def spread(p8, bins, first_bin, rows):
    n = p8.shape[1]
    row_bin = lax.broadcasted_iota(jnp.int32, (rows, n), 0) // 4 + first_bin
    mine = row_bin == bins
    hi = p8.astype(BF).astype(F32)
    lo = p8 - hi
    wide = lambda v: jnp.broadcast_to(v[None], (rows // 8, 8, n)).reshape(rows, n)
    return [jnp.where(mine, wide(v), 0.0).astype(BF) for v in (hi, lo)]


def add_sums(out_ref, rows, high, low, xh, xl, xr):
    main = jnp.dot(high, xh, preferred_element_type=F32)
    main = main + jnp.dot(low, xh, preferred_element_type=F32)
    main = main + jnp.dot(high, xl, preferred_element_type=F32)
    tail = jnp.dot(high, xr, preferred_element_type=F32) + jnp.dot(low, xr, preferred_element_type=F32)
    out_ref[rows, pl.ds(0, 256)] += main
    out_ref[rows, pl.ds(256, 128)] += tail


def sums_kernel(which, p_ref, tpl_ref, xh_ref, xl_ref, xr_ref, out_ref):
    step = pl.program_id(0)

    @pl.when(step == 0)
    def _():
        out_ref[...] = jnp.zeros_like(out_ref)

    half = lax.broadcasted_iota(jnp.int32, (8, 256), 0) < 4
    for side in range(2):
        first, second = side, 2 + side
        pair = lambda ref: jnp.concatenate([ref[first], ref[second]], axis=0)
        xh, xl, xr = pair(xh_ref), pair(xl_ref), pair(xr_ref)
        bins = bins_of(tpl_ref, 4 * step + first, 4 * step + second)
        if which == "halo":
            p8 = jnp.concatenate([p_ref[first, pl.ds(8, 8), :], p_ref[second, pl.ds(8, 8), :]], axis=1)
            for c in range(2):
                high, low = spread(p8, bins, 32 * c, 128)
                add_sums(out_ref, pl.ds(256 * side + 128 * c, 128), high, low, xh, xl, xr)
        else:
            own = jnp.concatenate([p_ref[first, pl.ds(0, 8), :], p_ref[second, pl.ds(0, 8), :]], axis=1)
            other = pltpu.roll(own, 4, 0)
            for k, p8 in enumerate((jnp.where(half, own, other), jnp.where(half, other, own))):
                for c in range(2):
                    high, low = spread(p8, bins, 32 * c, 128)
                    add_sums(out_ref, pl.ds(256 * k + 128 * c, 128), high, low, xh, xl, xr)


def sums(which, p, tpl, xh, xl, xr):
    n = xh.shape[0]
    whole = lambda shape: pl.BlockSpec(shape, lambda i: (0,) * len(shape))
    block = lambda *shape: pl.BlockSpec(shape, lambda i: (i,) + (0,) * (len(shape) - 1))

    def body(*refs):
        sums_kernel(which, *refs)

    return pl.pallas_call(
        body,
        grid=(n // 4,),
        in_specs=[block(4, 16, 128), whole((n, TPL, LANES)), block(4, 128, 256), block(4, 128, 256), block(4, 128, 128)],
        out_specs=whole((512, 384)),
        out_shape=jax.ShapeDtypeStruct((512, 384), F32),
        compiler_params=params(24),
        cost_estimate=cost(4_000_000_000, 6_000_000),
        name="sums_" + which,
    )(p, tpl, xh, xl, xr)


def average_kernel(own_ref, below_ref, above_ref, sq_ref, out_ref):
    for side, other_ref in ((0, below_ref), (1, above_ref)):
        for c in range(4):
            rows = pl.ds(64 * c, 64)
            total = own_ref[pl.ds(256 * side + 64 * c, 64), :] + other_ref[rows, :]
            weight = jnp.dot(total[:, 256:], sq_ref[...], precision=HIGHEST, preferred_element_type=F32)
            tail = total[:, 256:]
            tail = tail + pltpu.roll(tail, 96, 1)
            mean = jnp.concatenate([total[:, :256], tail], axis=1) / (weight + 1.0)
            for d in range(4):
                dest = 2 * (4 * c + d) + side
                piece = mean[16 * d : 16 * d + 16]
                out_ref[dest, pl.ds(0, 16), :] = piece[:, :128]
                out_ref[dest, pl.ds(16, 16), :] = piece[:, 128:256]
                rem = [piece[4 * b : 4 * b + 4, 256:] for b in range(4)]
                out_ref[dest, pl.ds(32, 4), :] = pick_groups([turned(rem[b], b) for b in range(4)])
                out_ref[dest, pl.ds(36, 4), :] = jnp.zeros((4, LANES), F32)


def averages(own, below, above, squares, n):
    vmem = pl.BlockSpec(memory_space=pltpu.VMEM)
    return pl.pallas_call(
        average_kernel,
        in_specs=[vmem] * 4,
        out_specs=vmem,
        out_shape=jax.ShapeDtypeStruct((n, 40, LANES), F32),
        compiler_params=params(8),
        cost_estimate=cost(200_000_000, 3_000_000),
        name="averages",
    )(own, below, above, squares)


def unpack_kernel(got_ref, out_ref):
    n = got_ref.shape[0]
    for i in range(n):
        for j in range(2):
            for b in range(4):
                out_ref[b, :, pl.ds(256 * i + 128 * j, 128)] = got_ref[i, pl.ds(16 * j + 4 * b, 4), :]
    for t in range(n // 4):
        rem = [got_ref[4 * t + q, pl.ds(32, 4), :] for q in range(4)]
        for b in range(4):
            out_ref[b, :, pl.ds(256 * n + 128 * t, 128)] = pick_groups([turned(rem[q], q - b) for q in range(4)])


def unpack(got, pixels):
    vmem = pl.BlockSpec(memory_space=pltpu.VMEM)
    return pl.pallas_call(
        unpack_kernel,
        in_specs=[vmem],
        out_specs=vmem,
        out_shape=jax.ShapeDtypeStruct((4, 4, pixels), F32),
        compiler_params=params(8),
        cost_estimate=cost(0, 1_200_000),
        name="unpack",
    )(got)


def exchange(value):
    return lax.all_to_all(value, PLANE, split_axis=0, concat_axis=0, tiled=True)


def along_z(value, by):
    size = lax.axis_size("z")
    return lax.ppermute(value, "z", [(i, (i + by) % size) for i in range(size)])


def local(images, prior_bin, prior_center, defocus_class, templates, ctf_table):
    pixels = images.shape[1]
    xlo = lax.axis_index("xlo")
    chunk = lax.axis_index("dir") * 2 + xlo
    first = lax.axis_index("z") * 8
    meta = jnp.stack([prior_bin, prior_center, defocus_class, defocus_class]).astype(F32)
    ctf_main = lax.dynamic_slice(ctf_table, (0, 256 * chunk), (CLASSES, 256))
    ctf_rem = lax.dynamic_slice(ctf_table, (0, 8192 + 32 * chunk), (CLASSES, 32))
    eye = jnp.eye(CLASSES, dtype=F32)
    ctf_ext = jnp.concatenate([ctf_main, ctf_rem, ctf_rem, ctf_rem, eye, eye], axis=1)
    square = jnp.concatenate([ctf_main, ctf_rem], axis=1)
    square = square * square
    to_class = jnp.pad(jnp.concatenate([square.T, square.T], axis=1), ((0, 96), (96, 0)))
    to_pixel = jnp.pad(square, ((96, 16), (0, 96)))

    buf = exchange(pack(images, templates, meta))
    n = buf.shape[0]
    tpl = buf[:, IMG:]
    sides = tpl.reshape(n // 2, 2, TPL, LANES)
    below = along_z(sides[:, 1], 1)
    above = along_z(sides[:, 0], -1)
    halo = jnp.concatenate([below, above], axis=0)
    xh, xl, xr, own = own_scores(buf, tpl, ctf_ext, to_class)
    partial = halo_scores(xh, xl, xr, own, tpl, halo, to_class)
    place = jnp.stack([xlo, first]).astype(jnp.int32)
    log_total, mean_shift, p = home(place, exchange(partial), prior_center[None])
    p = exchange(p)
    edge = sums("halo", p, tpl, xh, xl, xr)
    from_above = along_z(edge[:256], -1)
    from_below = along_z(edge[256:], 1)
    mine = sums("own", p, tpl, xh, xl, xr)
    out = averages(mine, from_below, from_above, to_pixel, n)
    average = unpack(exchange(out), pixels)
    return log_total[0], mean_shift[0], average


def solution(mesh):
    dirs, psis = mesh.devices.shape
    fine = Mesh(mesh.devices.reshape(dirs, psis // 2, 2), ("dir", "z", "xlo"))
    rows = P(("dir", "z", "xlo"))
    grid = P("dir", ("z", "xlo"), None)
    return jax.shard_map(
        local,
        mesh=fine,
        in_specs=(P(("dir", "z", "xlo"), None), rows, rows, rows, grid, P()),
        out_specs=(rows, rows, grid),
        check_vma=False,
    )
```

```python
import jax
import jax.numpy as jnp
from jax import lax
from jax.experimental import pallas as pl
from jax.experimental.pallas import tpu as pltpu
from jax.sharding import Mesh
from jax.sharding import PartitionSpec as P

HALF = 4
LANES = 128
CLASSES = 16
IMG = 288
TPL = 40
META = 36
BF = jnp.bfloat16
F32 = jnp.float32
HIGHEST = lax.Precision.HIGHEST
PLANE = ("dir", "xlo")


def params(mib):
    return pltpu.CompilerParams(vmem_limit_bytes=mib * 1024 * 1024)


def cost(flops, moved):
    return pl.CostEstimate(flops=flops, bytes_accessed=moved, transcendentals=0)


def lane_group(shape):
    return lax.broadcasted_iota(jnp.int32, shape, len(shape) - 1) // 32


def turned(x, groups):
    groups = groups % 4
    return x if groups == 0 else pltpu.roll(x, 32 * groups, x.ndim - 1)


def pick_groups(parts):
    group = lane_group(parts[0].shape)
    out = parts[3]
    for q in (2, 1, 0):
        out = jnp.where(group == q, parts[q], out)
    return out


def split(x):
    hi = x.astype(BF)
    return hi, (x - hi.astype(F32)).astype(BF)


def pack_images_kernel(img_ref, rem_ref, out_ref):
    for q in range(4):
        for j in range(2):
            out_ref[q, pl.ds(j * 128, 128), :] = img_ref[:, pl.ds((2 * q + j) * LANES, LANES)]
        out_ref[q, pl.ds(256, 32), :] = pick_groups([turned(rem_ref[pl.ds(32 * g, 32), :], g - q) for g in range(4)])


def pack_images(images):
    steps = 8
    return pl.pallas_call(
        pack_images_kernel,
        grid=(steps,),
        in_specs=[
            pl.BlockSpec((128, 1024), lambda t: (0, t)),
            pl.BlockSpec((128, LANES), lambda t: (0, 64 + t)),
        ],
        out_specs=pl.BlockSpec((4, IMG, LANES), lambda t: (t, 0, 0)),
        out_shape=jax.ShapeDtypeStruct((4 * steps, IMG, LANES), F32),
        compiler_params=params(60),
        cost_estimate=cost(0, 9_500_000),
        name="pack_images",
    )(images, images)


def pack_templates_kernel(tpl_ref, meta_ref, out_ref):
    meta = meta_ref[...]
    for t in range(8):
        rem = [tpl_ref[b, :, pl.ds((64 + t) * LANES, LANES)] for b in range(4)]
        for q in range(4):
            dest = 4 * t + q
            for j in range(2):
                for b in range(4):
                    out_ref[dest, pl.ds(16 * j + 4 * b, 4), :] = tpl_ref[b, :, pl.ds((2 * dest + j) * LANES, LANES)]
            out_ref[dest, pl.ds(32, 4), :] = pick_groups([turned(rem[b], b - q) for b in range(4)])
            out_ref[dest, pl.ds(META, 4), :] = meta


def pack_templates(templates, meta):
    vmem = pl.BlockSpec(memory_space=pltpu.VMEM)
    return pl.pallas_call(
        pack_templates_kernel,
        in_specs=[vmem, vmem],
        out_specs=vmem,
        out_shape=jax.ShapeDtypeStruct((32, TPL, LANES), F32),
        compiler_params=params(8),
        cost_estimate=cost(0, 1_300_000),
        name="pack_templates",
    )(templates, meta)


def operands_kernel(tpl_ref, below_ref, above_ref, ctf_ref, sq_ref, y_ref, ce_ref, tf_ref):
    for block in range(4):
        for d in range(16):
            at = lambda rows: (below_ref, tpl_ref, tpl_ref, above_ref)[block][(d, 2 * d, 2 * d + 1, d)[block], rows, :]
            rows = pl.ds(16 * d, 16)
            tf_ref[rows, pl.ds(0, 128)] = at(pl.ds(0, 16))
            tf_ref[rows, pl.ds(128, 128)] = at(pl.ds(16, 16))
            packed = at(pl.ds(32, 4))
            v = [turned(packed, j) for j in range(4)]
            for b in range(4):
                tail = pick_groups([v[(q - b) % 4] for q in (0, 1, 2)] + [jnp.zeros_like(packed)])
                tf_ref[pl.ds(16 * d + 4 * b, 4), pl.ds(256, 128)] = tail
        for c in range(4):
            out = pl.ds(256 * block + 64 * c, 64)
            full = tf_ref[pl.ds(64 * c, 64), :]
            quad = jnp.dot(full * full, sq_ref[...], precision=HIGHEST, preferred_element_type=F32)
            hi, lo = split(full)
            vh, vl = split(-0.5 * quad)
            lane = lax.broadcasted_iota(jnp.int32, (64, LANES), 1)
            last = jnp.where(lane < 112, vh.astype(F32), vl.astype(F32))
            tail = jnp.where(lane < 64, hi[:, 256:].astype(F32), lo[:, 256:].astype(F32))
            y_ref[out, pl.ds(0, 256)] = hi[:, :256]
            y_ref[out, pl.ds(256, 256)] = lo[:, :256]
            y_ref[out, pl.ds(512, 256)] = hi[:, :256]
            y_ref[out, pl.ds(768, 128)] = jnp.where(lane < 96, tail, last).astype(BF)
    ctf = ctf_ref[...]
    hi, mid = split(ctf)
    ce_ref[pl.ds(0, 16), :] = hi
    ce_ref[pl.ds(16, 16), :] = mid
    ce_ref[pl.ds(32, 16), :] = (ctf - hi.astype(F32) - mid.astype(F32)).astype(BF)


def operands(tpl, below, above, ctf_ext, squares):
    vmem = pl.BlockSpec(memory_space=pltpu.VMEM)
    return pl.pallas_call(
        operands_kernel,
        in_specs=[vmem] * 5,
        out_specs=[vmem, vmem],
        out_shape=[jax.ShapeDtypeStruct((1024, 896), BF), jax.ShapeDtypeStruct((48, 384), BF)],
        scratch_shapes=[pltpu.VMEM((256, 384), F32)],
        compiler_params=params(12),
        cost_estimate=cost(600_000_000, 4_000_000),
        name="operands",
    )(tpl, below, above, ctf_ext, squares)


def bins_of(tpl_ref, sources):
    rows = [tpl_ref[s, pl.ds(META, 1), :] for s in sources]
    return jnp.concatenate(rows, axis=1).astype(jnp.int32)


def scores_kernel(buf_ref, tpl_ref, y_ref, ce_ref, xh_ref, xl_ref, xr_ref, out_ref):
    step = pl.program_id(0)
    group = lane_group((128, LANES))
    for s in range(4):
        source = 4 * step + s
        classes = tpl_ref[source, pl.ds(META + 2, 1), :].astype(jnp.int32)
        row_class = lax.broadcasted_iota(jnp.int32, (48, 128), 0) % CLASSES
        onehot = jnp.where(row_class == classes, 1.0, 0.0).astype(BF)
        ctf = lax.dot_general(onehot, ce_ref[...], (((0,), (0,)), ((), ())), preferred_element_type=F32)
        for j in range(2):
            hi, lo = split(ctf[:, 128 * j : 128 * j + 128] * buf_ref[s, pl.ds(128 * j, 128), :])
            xh_ref[s, :, pl.ds(128 * j, 128)] = hi
            xl_ref[s, :, pl.ds(128 * j, 128)] = lo
        packed = buf_ref[s, pl.ds(256, 32), :]
        v = [turned(packed, j) for j in range(4)]
        one = jnp.ones_like(packed)
        rem = jnp.concatenate([pick_groups([v[(q - g) % 4] for q in (0, 1, 2)] + [one]) for g in range(4)], axis=0)
        hi, lo = split(ctf[:, 256:] * rem)
        xr_ref[s, :, :] = jnp.where(group == 1, lo.astype(F32), hi.astype(F32)).astype(BF)
    row_bin = lax.broadcasted_iota(jnp.int32, (256, 256), 0) // 4
    half = lax.broadcasted_iota(jnp.int32, (8, 256), 0) < 4
    for side in range(2):
        pair = (side, 2 + side)
        x = jnp.concatenate(
            [jnp.concatenate([xh_ref[s], xh_ref[s], xl_ref[s], xr_ref[s]], axis=1) for s in pair], axis=0
        )
        mine = row_bin == bins_of(tpl_ref, [4 * step + s for s in pair])
        all_rows = lax.dot_general(
            y_ref[pl.ds(256 * side, 768), :], x, (((1,), (1,)), ((), ())), preferred_element_type=F32
        )
        blocks = []
        for k in range(3):
            kept = jnp.where(mine, all_rows[256 * k : 256 * k + 256], 0.0)
            total = jnp.sum(kept.reshape(32, 8, 256), axis=0)
            blocks.append(total + pltpu.roll(total, 4, 0))
        edge, low, high = blocks if side == 0 else (blocks[2], blocks[0], blocks[1])
        own = jnp.where(half, low, high)
        for k, s in enumerate(pair):
            cols = slice(128 * k, 128 * k + 128)
            out_ref[s, pl.ds(0, 8), :] = own[:, cols]
            out_ref[s, pl.ds(8, 8), :] = edge[:, cols]


def window_scores(buf, tpl, y, ctf):
    n = buf.shape[0]
    whole = lambda shape: pl.BlockSpec(shape, lambda p: (0,) * len(shape))
    block = lambda *shape: pl.BlockSpec(shape, lambda p: (p,) + (0,) * (len(shape) - 1))
    return pl.pallas_call(
        scores_kernel,
        grid=(n // 4,),
        in_specs=[block(4, IMG, LANES), whole((n, TPL, LANES)), whole((1024, 896)), whole((48, 384))],
        out_specs=[block(4, 128, 256), block(4, 128, 256), block(4, 128, 128), block(4, 16, 128)],
        out_shape=[
            jax.ShapeDtypeStruct((n, 128, 256), BF),
            jax.ShapeDtypeStruct((n, 128, 256), BF),
            jax.ShapeDtypeStruct((n, 128, 128), BF),
            jax.ShapeDtypeStruct((n, 16, 128), F32),
        ],
        compiler_params=params(60),
        cost_estimate=cost(6_000_000_000, 14_000_000),
        name="window_scores",
    )(buf, tpl, y, ctf)


def home_kernel(place_ref, scores_ref, centre_ref, total_ref, shift_ref, p_ref):
    xlo = place_ref[0]
    first = place_ref[1]
    n = scores_ref.shape[0]
    scores = scores_ref[0]
    for s in range(1, n):
        scores = scores + scores_ref[s]
    row = lax.broadcasted_iota(jnp.int32, scores.shape, 0)
    angle = jnp.where(row < 8, row + 4, row - 8 + 12 * xlo)
    offset = angle - (centre_ref[...] - first + 4)
    inside = jnp.logical_and(jnp.abs(offset) <= HALF, row < 12)
    safe = jnp.where(inside, scores, 0.0)
    total = jnp.log(jnp.sum(jnp.where(inside, jnp.exp(safe), 0.0), axis=0, keepdims=True))
    p = jnp.where(inside, jnp.exp(safe - total), 0.0)
    total_ref[...] = total
    shift_ref[...] = jnp.sum(p * offset.astype(F32), axis=0, keepdims=True)
    p = jnp.where(row < 12, p, pltpu.roll(p, 4, 0))
    for s in range(n):
        p_ref[s] = p


def home(place, scores, centre):
    n = scores.shape[0]
    vmem = pl.BlockSpec(memory_space=pltpu.VMEM)
    return pl.pallas_call(
        home_kernel,
        in_specs=[pl.BlockSpec(memory_space=pltpu.SMEM), vmem, vmem],
        out_specs=[vmem, vmem, vmem],
        out_shape=[
            jax.ShapeDtypeStruct((1, 128), F32),
            jax.ShapeDtypeStruct((1, 128), F32),
            jax.ShapeDtypeStruct((n, 16, 128), F32),
        ],
        compiler_params=params(4),
        cost_estimate=cost(200_000, 600_000),
        name="home",
    )(place, scores, centre)


def spread(p8, bins, first_bin, rows):
    n = p8.shape[1]
    row_bin = lax.broadcasted_iota(jnp.int32, (rows, n), 0) // 4 + first_bin
    mine = row_bin == bins
    hi = p8.astype(BF).astype(F32)
    lo = p8 - hi
    wide = lambda v: jnp.broadcast_to(v[None], (rows // 8, 8, n)).reshape(rows, n)
    return [jnp.where(mine, wide(v), 0.0).astype(BF) for v in (hi, lo)]


def sums_kernel(which, p_ref, tpl_ref, xh_ref, xl_ref, xr_ref, out_ref):
    step = pl.program_id(0)

    @pl.when(step == 0)
    def _():
        out_ref[...] = jnp.zeros_like(out_ref)

    def add(rows, high, low, sources):
        stack = lambda ref: jnp.concatenate([ref[s] for s in sources], axis=0)
        xh, xl, xr = stack(xh_ref), stack(xl_ref), stack(xr_ref)
        left = jnp.concatenate([high, low, high], axis=1)
        main = jnp.dot(left, jnp.concatenate([xh, xh, xl], axis=0), preferred_element_type=F32)
        wide = left.shape[1] // 3 * 2
        tail = jnp.dot(left[:, :wide], jnp.concatenate([xr, xr], axis=0), preferred_element_type=F32)
        out_ref[rows, pl.ds(0, 256)] += main
        out_ref[rows, pl.ds(256, 128)] += tail

    if which == "halo":
        for side in range(2):
            pair = (side, 2 + side)
            p8 = jnp.concatenate([p_ref[s, pl.ds(8, 8), :] for s in pair], axis=1)
            high, low = spread(p8, bins_of(tpl_ref, [4 * step + s for s in pair]), 0, 256)
            add(pl.ds(256 * side, 256), high, low, pair)
    else:
        four = range(4)
        half = lax.broadcasted_iota(jnp.int32, (8, 512), 0) < 4
        bins = bins_of(tpl_ref, [4 * step + s for s in four])
        own = jnp.concatenate([p_ref[s, pl.ds(0, 8), :] for s in four], axis=1)
        other = pltpu.roll(own, 4, 0)
        for k, p8 in enumerate((jnp.where(half, own, other), jnp.where(half, other, own))):
            high, low = spread(p8, bins, 0, 256)
            add(pl.ds(256 * k, 256), high, low, four)


def sums(which, p, tpl, xh, xl, xr):
    n = xh.shape[0]
    whole = lambda shape: pl.BlockSpec(shape, lambda i: (0,) * len(shape))
    block = lambda *shape: pl.BlockSpec(shape, lambda i: (i,) + (0,) * (len(shape) - 1))

    def body(*refs):
        sums_kernel(which, *refs)

    return pl.pallas_call(
        body,
        grid=(n // 4,),
        in_specs=[block(4, 16, 128), whole((n, TPL, LANES)), block(4, 128, 256), block(4, 128, 256), block(4, 128, 128)],
        out_specs=whole((512, 384)),
        out_shape=jax.ShapeDtypeStruct((512, 384), F32),
        compiler_params=params(60),
        cost_estimate=cost(4_000_000_000, 6_000_000),
        name="sums_" + which,
    )(p, tpl, xh, xl, xr)


def average_kernel(own_ref, below_ref, above_ref, sq_ref, out_ref):
    for side, other_ref in ((0, below_ref), (1, above_ref)):
        for c in range(4):
            rows = pl.ds(64 * c, 64)
            total = own_ref[pl.ds(256 * side + 64 * c, 64), :] + other_ref[rows, :]
            weight = jnp.dot(total[:, 256:], sq_ref[...], precision=HIGHEST, preferred_element_type=F32)
            tail = total[:, 256:]
            tail = tail + pltpu.roll(tail, 96, 1)
            mean = jnp.concatenate([total[:, :256], tail], axis=1) / (weight + 1.0)
            for d in range(4):
                dest = 2 * (4 * c + d) + side
                piece = mean[16 * d : 16 * d + 16]
                out_ref[dest, pl.ds(0, 16), :] = piece[:, :128]
                out_ref[dest, pl.ds(16, 16), :] = piece[:, 128:256]
                rem = [piece[4 * b : 4 * b + 4, 256:] for b in range(4)]
                out_ref[dest, pl.ds(32, 4), :] = pick_groups([turned(rem[b], b) for b in range(4)])
                out_ref[dest, pl.ds(36, 4), :] = jnp.zeros((4, LANES), F32)


def averages(own, below, above, squares, n):
    vmem = pl.BlockSpec(memory_space=pltpu.VMEM)
    return pl.pallas_call(
        average_kernel,
        in_specs=[vmem] * 4,
        out_specs=vmem,
        out_shape=jax.ShapeDtypeStruct((n, 40, LANES), F32),
        compiler_params=params(8),
        cost_estimate=cost(200_000_000, 3_000_000),
        name="averages",
    )(own, below, above, squares)


def unpack_kernel(got_ref, out_ref):
    n = got_ref.shape[0]
    for i in range(n):
        for j in range(2):
            for b in range(4):
                out_ref[b, :, pl.ds(256 * i + 128 * j, 128)] = got_ref[i, pl.ds(16 * j + 4 * b, 4), :]
    for t in range(n // 4):
        rem = [got_ref[4 * t + q, pl.ds(32, 4), :] for q in range(4)]
        for b in range(4):
            out_ref[b, :, pl.ds(256 * n + 128 * t, 128)] = pick_groups([turned(rem[q], q - b) for q in range(4)])


def unpack(got, pixels):
    vmem = pl.BlockSpec(memory_space=pltpu.VMEM)
    return pl.pallas_call(
        unpack_kernel,
        in_specs=[vmem],
        out_specs=vmem,
        out_shape=jax.ShapeDtypeStruct((4, 4, pixels), F32),
        compiler_params=params(8),
        cost_estimate=cost(0, 1_200_000),
        name="unpack",
    )(got)


def exchange(value):
    return lax.all_to_all(value, PLANE, split_axis=0, concat_axis=0, tiled=True)


def along_z(value, by):
    size = lax.axis_size("z")
    return lax.ppermute(value, "z", [(i, (i + by) % size) for i in range(size)])


def local(images, prior_bin, prior_center, defocus_class, templates, ctf_table):
    pixels = images.shape[1]
    xlo = lax.axis_index("xlo")
    chunk = lax.axis_index("dir") * 2 + xlo
    first = lax.axis_index("z") * 8
    meta = jnp.stack([prior_bin, prior_center, defocus_class, defocus_class]).astype(F32)
    ctf_main = lax.dynamic_slice(ctf_table, (0, 256 * chunk), (CLASSES, 256))
    ctf_rem = lax.dynamic_slice(ctf_table, (0, 8192 + 32 * chunk), (CLASSES, 32))
    eye = jnp.eye(CLASSES, dtype=F32)
    ctf_ext = jnp.concatenate([ctf_main, ctf_rem, ctf_rem, ctf_rem, eye, eye], axis=1)
    square = jnp.concatenate([ctf_main, ctf_rem], axis=1)
    square = square * square
    to_class = jnp.pad(jnp.concatenate([square.T, square.T], axis=1), ((0, 96), (96, 0)))
    to_pixel = jnp.pad(square, ((96, 16), (0, 96)))

    tpl = exchange(pack_templates(templates, meta))
    n = tpl.shape[0]
    buf = exchange(pack_images(images))
    sides = tpl.reshape(n // 2, 2, TPL, LANES)
    below = along_z(sides[:, 1], 1)
    above = along_z(sides[:, 0], -1)
    y, ctf = operands(tpl, below, above, ctf_ext, to_class)
    xh, xl, xr, partial = window_scores(buf, tpl, y, ctf)
    place = jnp.stack([xlo, first]).astype(jnp.int32)
    log_total, mean_shift, p = home(place, exchange(partial), prior_center[None])
    p = exchange(p)
    edge = sums("halo", p, tpl, xh, xl, xr)
    from_above = along_z(edge[:256], -1)
    from_below = along_z(edge[256:], 1)
    mine = sums("own", p, tpl, xh, xl, xr)
    out = averages(mine, from_below, from_above, to_pixel, n)
    average = unpack(exchange(out), pixels)
    return log_total[0], mean_shift[0], average


def solution(mesh):
    dirs, psis = mesh.devices.shape
    fine = Mesh(mesh.devices.reshape(dirs, psis // 2, 2), ("dir", "z", "xlo"))
    rows = P(("dir", "z", "xlo"))
    grid = P("dir", ("z", "xlo"), None)
    return jax.shard_map(
        local,
        mesh=fine,
        in_specs=(P(("dir", "z", "xlo"), None), rows, rows, rows, grid, P()),
        out_specs=(rows, rows, grid),
        check_vma=False,
    )
```

```python
import jax
import jax.numpy as jnp
from jax import lax
from jax.experimental import pallas as pl
from jax.experimental.pallas import tpu as pltpu
from jax.sharding import Mesh
from jax.sharding import PartitionSpec as P

HALF = 4
LANES = 128
CLASSES = 16
IMG = 288
TPL = 40
META = 36
BF = jnp.bfloat16
F32 = jnp.float32
HIGHEST = lax.Precision.HIGHEST
PLANE = ("dir", "xlo")


def params(mib):
    return pltpu.CompilerParams(vmem_limit_bytes=mib * 1024 * 1024)


def cost(flops, moved):
    return pl.CostEstimate(flops=flops, bytes_accessed=moved, transcendentals=0)


def lane_group(shape):
    return lax.broadcasted_iota(jnp.int32, shape, len(shape) - 1) // 32


def turned(x, groups):
    groups = groups % 4
    return x if groups == 0 else pltpu.roll(x, 32 * groups, x.ndim - 1)


def pick_groups(parts):
    group = lane_group(parts[0].shape)
    out = parts[3]
    for q in (2, 1, 0):
        out = jnp.where(group == q, parts[q], out)
    return out


def split(x):
    hi = x.astype(BF)
    return hi, (x - hi.astype(F32)).astype(BF)


def pack_images_kernel(img_ref, rem_ref, out_ref):
    for q in range(4):
        for j in range(2):
            out_ref[q, pl.ds(j * 128, 128), :] = img_ref[:, pl.ds((2 * q + j) * LANES, LANES)]
        out_ref[q, pl.ds(256, 32), :] = pick_groups([turned(rem_ref[pl.ds(32 * g, 32), :], g - q) for g in range(4)])


def pack_images(images):
    steps = 8
    return pl.pallas_call(
        pack_images_kernel,
        grid=(steps,),
        in_specs=[
            pl.BlockSpec((128, 1024), lambda t: (0, t)),
            pl.BlockSpec((128, LANES), lambda t: (0, 64 + t)),
        ],
        out_specs=pl.BlockSpec((4, IMG, LANES), lambda t: (t, 0, 0)),
        out_shape=jax.ShapeDtypeStruct((4 * steps, IMG, LANES), F32),
        compiler_params=params(60),
        cost_estimate=cost(0, 9_500_000),
        name="pack_images",
    )(images, images)


def pack_templates_kernel(tpl_ref, rem_ref, bin_ref, class_ref, out_ref):
    bins = bin_ref[...].astype(F32)
    classes = class_ref[...].astype(F32)
    rem = [rem_ref[b] for b in range(4)]
    for q in range(4):
        for j in range(2):
            for b in range(4):
                out_ref[q, pl.ds(16 * j + 4 * b, 4), :] = tpl_ref[b, :, pl.ds((2 * q + j) * LANES, LANES)]
        out_ref[q, pl.ds(32, 4), :] = pick_groups([turned(rem[b], b - q) for b in range(4)])
        out_ref[q, pl.ds(META, 2), :] = jnp.broadcast_to(bins, (2, LANES))
        out_ref[q, pl.ds(META + 2, 2), :] = jnp.broadcast_to(classes, (2, LANES))


def pack_templates(templates, bins, classes):
    steps = 8
    one = pl.BlockSpec((1, LANES), lambda t: (0, 0))
    return pl.pallas_call(
        pack_templates_kernel,
        grid=(steps,),
        in_specs=[
            pl.BlockSpec((4, 4, 1024), lambda t: (0, 0, t)),
            pl.BlockSpec((4, 4, LANES), lambda t: (0, 0, 64 + t)),
            one,
            one,
        ],
        out_specs=pl.BlockSpec((4, TPL, LANES), lambda t: (t, 0, 0)),
        out_shape=jax.ShapeDtypeStruct((4 * steps, TPL, LANES), F32),
        compiler_params=params(60),
        cost_estimate=cost(0, 1_300_000),
        name="pack_templates",
    )(templates, templates, bins, classes)


def operands_kernel(tpl_ref, below_ref, above_ref, ctf_ref, sq_ref, y_ref, ce_ref, tf_ref):
    for block in range(4):
        for d in range(16):
            at = lambda rows: (below_ref, tpl_ref, tpl_ref, above_ref)[block][(d, 2 * d, 2 * d + 1, d)[block], rows, :]
            rows = pl.ds(16 * d, 16)
            tf_ref[rows, pl.ds(0, 128)] = at(pl.ds(0, 16))
            tf_ref[rows, pl.ds(128, 128)] = at(pl.ds(16, 16))
            packed = at(pl.ds(32, 4))
            v = [turned(packed, j) for j in range(4)]
            for b in range(4):
                tail = pick_groups([v[(q - b) % 4] for q in (0, 1, 2)] + [jnp.zeros_like(packed)])
                tf_ref[pl.ds(16 * d + 4 * b, 4), pl.ds(256, 128)] = tail
        for c in range(4):
            out = pl.ds(256 * block + 64 * c, 64)
            full = tf_ref[pl.ds(64 * c, 64), :]
            quad = jnp.dot(full * full, sq_ref[...], precision=HIGHEST, preferred_element_type=F32)
            hi, lo = split(full)
            vh, vl = split(-0.5 * quad)
            lane = lax.broadcasted_iota(jnp.int32, (64, LANES), 1)
            last = jnp.where(lane < 112, vh.astype(F32), vl.astype(F32))
            tail = jnp.where(lane < 64, hi[:, 256:].astype(F32), lo[:, 256:].astype(F32))
            y_ref[out, pl.ds(0, 256)] = hi[:, :256]
            y_ref[out, pl.ds(256, 256)] = lo[:, :256]
            y_ref[out, pl.ds(512, 128)] = jnp.where(lane < 96, tail, last).astype(BF)
    ctf = ctf_ref[...]
    hi, mid = split(ctf)
    ce_ref[pl.ds(0, 16), :] = hi
    ce_ref[pl.ds(16, 16), :] = mid
    ce_ref[pl.ds(32, 16), :] = (ctf - hi.astype(F32) - mid.astype(F32)).astype(BF)


def operands(tpl, below, above, ctf_ext, squares):
    vmem = pl.BlockSpec(memory_space=pltpu.VMEM)
    return pl.pallas_call(
        operands_kernel,
        in_specs=[vmem] * 5,
        out_specs=[vmem, vmem],
        out_shape=[jax.ShapeDtypeStruct((1024, 640), BF), jax.ShapeDtypeStruct((48, 384), BF)],
        scratch_shapes=[pltpu.VMEM((256, 384), F32)],
        compiler_params=params(12),
        cost_estimate=cost(600_000_000, 4_000_000),
        name="operands",
    )(tpl, below, above, ctf_ext, squares)


def bins_of(tpl_ref, sources):
    rows = [tpl_ref[s, pl.ds(META, 1), :] for s in sources]
    return jnp.concatenate(rows, axis=1).astype(jnp.int32)


def scores_kernel(buf_ref, tpl_ref, y_ref, ce_ref, xh_ref, xl_ref, xr_ref, out_ref):
    step = pl.program_id(0)
    group = lane_group((128, LANES))
    for s in range(4):
        source = 4 * step + s
        classes = tpl_ref[source, pl.ds(META + 2, 1), :].astype(jnp.int32)
        row_class = lax.broadcasted_iota(jnp.int32, (48, 128), 0) % CLASSES
        onehot = jnp.where(row_class == classes, 1.0, 0.0).astype(BF)
        ctf = lax.dot_general(onehot, ce_ref[...], (((0,), (0,)), ((), ())), preferred_element_type=F32)
        for j in range(2):
            hi, lo = split(ctf[:, 128 * j : 128 * j + 128] * buf_ref[s, pl.ds(128 * j, 128), :])
            xh_ref[s, :, pl.ds(128 * j, 128)] = hi
            xl_ref[s, :, pl.ds(128 * j, 128)] = lo
        packed = buf_ref[s, pl.ds(256, 32), :]
        v = [turned(packed, j) for j in range(4)]
        one = jnp.ones_like(packed)
        rem = jnp.concatenate([pick_groups([v[(q - g) % 4] for q in (0, 1, 2)] + [one]) for g in range(4)], axis=0)
        hi, lo = split(ctf[:, 256:] * rem)
        xr_ref[s, :, :] = jnp.where(group == 1, lo.astype(F32), hi.astype(F32)).astype(BF)
    row_bin = lax.broadcasted_iota(jnp.int32, (256, 256), 0) // 4
    half = lax.broadcasted_iota(jnp.int32, (8, 256), 0) < 4
    for side in range(2):
        pair = (side, 2 + side)
        x = jnp.concatenate(
            [jnp.concatenate([xh_ref[s], xh_ref[s], xl_ref[s], xr_ref[s]], axis=1) for s in pair], axis=0
        )
        mine = row_bin == bins_of(tpl_ref, [4 * step + s for s in pair])
        y = y_ref[pl.ds(256 * side, 768), :]
        y = jnp.concatenate([y[:, :512], y[:, :256], y[:, 512:]], axis=1)
        all_rows = lax.dot_general(y, x, (((1,), (1,)), ((), ())), preferred_element_type=F32)
        blocks = []
        for k in range(3):
            kept = jnp.where(mine, all_rows[256 * k : 256 * k + 256], 0.0)
            total = jnp.sum(kept.reshape(32, 8, 256), axis=0)
            blocks.append(total + pltpu.roll(total, 4, 0))
        edge, low, high = blocks if side == 0 else (blocks[2], blocks[0], blocks[1])
        own = jnp.where(half, low, high)
        for k, s in enumerate(pair):
            cols = slice(128 * k, 128 * k + 128)
            out_ref[s, pl.ds(0, 8), :] = own[:, cols]
            out_ref[s, pl.ds(8, 8), :] = edge[:, cols]


def window_scores(buf, tpl, y, ctf):
    n = buf.shape[0]
    whole = lambda shape: pl.BlockSpec(shape, lambda p: (0,) * len(shape))
    block = lambda *shape: pl.BlockSpec(shape, lambda p: (p,) + (0,) * (len(shape) - 1))
    return pl.pallas_call(
        scores_kernel,
        grid=(n // 4,),
        in_specs=[block(4, IMG, LANES), whole((n, TPL, LANES)), whole((1024, 640)), whole((48, 384))],
        out_specs=[block(4, 128, 256), block(4, 128, 256), block(4, 128, 128), block(4, 16, 128)],
        out_shape=[
            jax.ShapeDtypeStruct((n, 128, 256), BF),
            jax.ShapeDtypeStruct((n, 128, 256), BF),
            jax.ShapeDtypeStruct((n, 128, 128), BF),
            jax.ShapeDtypeStruct((n, 16, 128), F32),
        ],
        compiler_params=params(24),
        cost_estimate=cost(6_000_000_000, 14_000_000),
        name="window_scores",
    )(buf, tpl, y, ctf)


def home_kernel(scores_ref, centre_ref, total_ref, shift_ref, p_ref):
    xlo = lax.axis_index("xlo")
    first = lax.axis_index("z") * 8
    n = scores_ref.shape[0]
    scores = scores_ref[0]
    for s in range(1, n):
        scores = scores + scores_ref[s]
    row = lax.broadcasted_iota(jnp.int32, scores.shape, 0)
    angle = jnp.where(row < 8, row + 4, row - 8 + 12 * xlo)
    offset = angle - (centre_ref[...] - first + 4)
    inside = jnp.logical_and(jnp.abs(offset) <= HALF, row < 12)
    safe = jnp.where(inside, scores, 0.0)
    total = jnp.log(jnp.sum(jnp.where(inside, jnp.exp(safe), 0.0), axis=0, keepdims=True))
    p = jnp.where(inside, jnp.exp(safe - total), 0.0)
    total_ref[...] = total
    shift_ref[...] = jnp.sum(p * offset.astype(F32), axis=0, keepdims=True)
    p = jnp.where(row < 12, p, pltpu.roll(p, 4, 0))
    for s in range(n):
        p_ref[s] = p


def home(scores, centre):
    n = scores.shape[0]
    vmem = pl.BlockSpec(memory_space=pltpu.VMEM)
    return pl.pallas_call(
        home_kernel,
        in_specs=[vmem, vmem],
        out_specs=[vmem, vmem, vmem],
        out_shape=[
            jax.ShapeDtypeStruct((1, 128), F32),
            jax.ShapeDtypeStruct((1, 128), F32),
            jax.ShapeDtypeStruct((n, 16, 128), F32),
        ],
        compiler_params=params(4),
        cost_estimate=cost(200_000, 600_000),
        name="home",
    )(scores, centre)


def spread(p8, bins, first_bin, rows):
    n = p8.shape[1]
    row_bin = lax.broadcasted_iota(jnp.int32, (rows, n), 0) // 4 + first_bin
    mine = row_bin == bins
    hi = p8.astype(BF).astype(F32)
    lo = p8 - hi
    wide = lambda v: jnp.broadcast_to(v[None], (rows // 8, 8, n)).reshape(rows, n)
    return [jnp.where(mine, wide(v), 0.0).astype(BF) for v in (hi, lo)]


def sums_kernel(which, p_ref, tpl_ref, xh_ref, xl_ref, xr_ref, out_ref):
    step = pl.program_id(0)

    @pl.when(step == 0)
    def _():
        out_ref[...] = jnp.zeros_like(out_ref)

    def add(rows, high, low, sources):
        stack = lambda ref: jnp.concatenate([ref[s] for s in sources], axis=0)
        xh, xl, xr = stack(xh_ref), stack(xl_ref), stack(xr_ref)
        left = jnp.concatenate([high, low, high], axis=1)
        main = jnp.dot(left, jnp.concatenate([xh, xh, xl], axis=0), preferred_element_type=F32)
        wide = left.shape[1] // 3 * 2
        tail = jnp.dot(left[:, :wide], jnp.concatenate([xr, xr], axis=0), preferred_element_type=F32)
        out_ref[rows, pl.ds(0, 256)] += main
        out_ref[rows, pl.ds(256, 128)] += tail

    if which == "halo":
        for side in range(2):
            pair = (side, 2 + side)
            p8 = jnp.concatenate([p_ref[s, pl.ds(8, 8), :] for s in pair], axis=1)
            high, low = spread(p8, bins_of(tpl_ref, [4 * step + s for s in pair]), 0, 256)
            add(pl.ds(256 * side, 256), high, low, pair)
    else:
        four = range(4)
        half = lax.broadcasted_iota(jnp.int32, (8, 512), 0) < 4
        bins = bins_of(tpl_ref, [4 * step + s for s in four])
        own = jnp.concatenate([p_ref[s, pl.ds(0, 8), :] for s in four], axis=1)
        other = pltpu.roll(own, 4, 0)
        for k, p8 in enumerate((jnp.where(half, own, other), jnp.where(half, other, own))):
            high, low = spread(p8, bins, 0, 256)
            add(pl.ds(256 * k, 256), high, low, four)


def sums(which, p, tpl, xh, xl, xr):
    n = xh.shape[0]
    whole = lambda shape: pl.BlockSpec(shape, lambda i: (0,) * len(shape))
    block = lambda *shape: pl.BlockSpec(shape, lambda i: (i,) + (0,) * (len(shape) - 1))

    def body(*refs):
        sums_kernel(which, *refs)

    return pl.pallas_call(
        body,
        grid=(n // 4,),
        in_specs=[block(4, 16, 128), whole((n, TPL, LANES)), block(4, 128, 256), block(4, 128, 256), block(4, 128, 128)],
        out_specs=whole((512, 384)),
        out_shape=jax.ShapeDtypeStruct((512, 384), F32),
        compiler_params=params(24),
        cost_estimate=cost(4_000_000_000, 6_000_000),
        name="sums_" + which,
    )(p, tpl, xh, xl, xr)


def average_kernel(own_ref, below_ref, above_ref, sq_ref, out_ref):
    for side, other_ref in ((0, below_ref), (1, above_ref)):
        for c in range(4):
            rows = pl.ds(64 * c, 64)
            total = own_ref[pl.ds(256 * side + 64 * c, 64), :] + other_ref[rows, :]
            weight = jnp.dot(total[:, 256:], sq_ref[...], precision=HIGHEST, preferred_element_type=F32)
            tail = total[:, 256:]
            tail = tail + pltpu.roll(tail, 96, 1)
            mean = jnp.concatenate([total[:, :256], tail], axis=1) / (weight + 1.0)
            for d in range(4):
                dest = 2 * (4 * c + d) + side
                piece = mean[16 * d : 16 * d + 16]
                out_ref[dest, pl.ds(0, 16), :] = piece[:, :128]
                out_ref[dest, pl.ds(16, 16), :] = piece[:, 128:256]
                rem = [piece[4 * b : 4 * b + 4, 256:] for b in range(4)]
                out_ref[dest, pl.ds(32, 4), :] = pick_groups([turned(rem[b], b) for b in range(4)])
                out_ref[dest, pl.ds(36, 4), :] = jnp.zeros((4, LANES), F32)


def averages(own, below, above, squares, n):
    vmem = pl.BlockSpec(memory_space=pltpu.VMEM)
    return pl.pallas_call(
        average_kernel,
        in_specs=[vmem] * 4,
        out_specs=vmem,
        out_shape=jax.ShapeDtypeStruct((n, 40, LANES), F32),
        compiler_params=params(8),
        cost_estimate=cost(200_000_000, 3_000_000),
        name="averages",
    )(own, below, above, squares)


def unpack_kernel(got_ref, out_ref):
    n = got_ref.shape[0]
    for i in range(n):
        for j in range(2):
            for b in range(4):
                out_ref[b, :, pl.ds(256 * i + 128 * j, 128)] = got_ref[i, pl.ds(16 * j + 4 * b, 4), :]
    for t in range(n // 4):
        rem = [got_ref[4 * t + q, pl.ds(32, 4), :] for q in range(4)]
        for b in range(4):
            out_ref[b, :, pl.ds(256 * n + 128 * t, 128)] = pick_groups([turned(rem[q], q - b) for q in range(4)])


def unpack(got, pixels):
    vmem = pl.BlockSpec(memory_space=pltpu.VMEM)
    return pl.pallas_call(
        unpack_kernel,
        in_specs=[vmem],
        out_specs=vmem,
        out_shape=jax.ShapeDtypeStruct((4, 4, pixels), F32),
        compiler_params=params(8),
        cost_estimate=cost(0, 1_200_000),
        name="unpack",
    )(got)


def exchange(value):
    return lax.all_to_all(value, PLANE, split_axis=0, concat_axis=0, tiled=True)


def along_z(value, by):
    size = lax.axis_size("z")
    return lax.ppermute(value, "z", [(i, (i + by) % size) for i in range(size)])


def local(images, prior_bin, prior_center, defocus_class, templates, ctf_table):
    pixels = images.shape[1]
    xlo = lax.axis_index("xlo")
    chunk = lax.axis_index("dir") * 2 + xlo
    ctf_main = lax.dynamic_slice(ctf_table, (0, 256 * chunk), (CLASSES, 256))
    ctf_rem = lax.dynamic_slice(ctf_table, (0, 8192 + 32 * chunk), (CLASSES, 32))
    eye = jnp.eye(CLASSES, dtype=F32)
    ctf_ext = jnp.concatenate([ctf_main, ctf_rem, ctf_rem, ctf_rem, eye, eye], axis=1)
    square = jnp.concatenate([ctf_main, ctf_rem], axis=1)
    square = square * square
    to_class = jnp.pad(jnp.concatenate([square.T, square.T], axis=1), ((0, 96), (96, 0)))
    to_pixel = jnp.pad(square, ((96, 16), (0, 96)))

    tpl = exchange(pack_templates(templates, prior_bin[None], defocus_class[None]))
    n = tpl.shape[0]
    buf = exchange(pack_images(images))
    sides = tpl.reshape(n // 2, 2, TPL, LANES)
    below = along_z(sides[:, 1], 1)
    above = along_z(sides[:, 0], -1)
    y, ctf = operands(tpl, below, above, ctf_ext, to_class)
    xh, xl, xr, partial = window_scores(buf, tpl, y, ctf)
    log_total, mean_shift, p = home(exchange(partial), prior_center[None])
    p = exchange(p)
    edge = sums("halo", p, tpl, xh, xl, xr)
    from_above = along_z(edge[:256], -1)
    from_below = along_z(edge[256:], 1)
    mine = sums("own", p, tpl, xh, xl, xr)
    out = averages(mine, from_below, from_above, to_pixel, n)
    average = unpack(exchange(out), pixels)
    return log_total[0], mean_shift[0], average


def solution(mesh):
    dirs, psis = mesh.devices.shape
    fine = Mesh(mesh.devices.reshape(dirs, psis // 2, 2), ("dir", "z", "xlo"))
    rows = P(("dir", "z", "xlo"))
    grid = P("dir", ("z", "xlo"), None)
    return jax.shard_map(
        local,
        mesh=fine,
        in_specs=(P(("dir", "z", "xlo"), None), rows, rows, rows, grid, P()),
        out_specs=(rows, rows, grid),
        check_vma=False,
    )
```

```python
import jax
import jax.numpy as jnp
from jax import lax
from jax.experimental import pallas as pl
from jax.experimental.pallas import tpu as pltpu
from jax.sharding import Mesh
from jax.sharding import PartitionSpec as P

HALF = 4
LANES = 128
CLASSES = 16
IMG = 288
TPL = 40
META = 36
BF = jnp.bfloat16
F32 = jnp.float32
HIGHEST = lax.Precision.HIGHEST
PLANE = ("dir", "xlo")


def params(mib):
    return pltpu.CompilerParams(vmem_limit_bytes=mib * 1024 * 1024)


def cost(flops, moved):
    return pl.CostEstimate(flops=flops, bytes_accessed=moved, transcendentals=0)


def lane_group(shape):
    return lax.broadcasted_iota(jnp.int32, shape, len(shape) - 1) // 32


def turned(x, groups):
    groups = groups % 4
    return x if groups == 0 else pltpu.roll(x, 32 * groups, x.ndim - 1)


def pick_groups(parts):
    group = lane_group(parts[0].shape)
    out = parts[3]
    for q in (2, 1, 0):
        out = jnp.where(group == q, parts[q], out)
    return out


def split(x):
    hi = x.astype(BF)
    return hi, (x - hi.astype(F32)).astype(BF)


def pack_images_kernel(img_ref, rem_ref, out_ref):
    for q in range(4):
        for j in range(2):
            out_ref[q, pl.ds(j * 128, 128), :] = img_ref[:, pl.ds((2 * q + j) * LANES, LANES)]
        out_ref[q, pl.ds(256, 32), :] = pick_groups([turned(rem_ref[pl.ds(32 * g, 32), :], g - q) for g in range(4)])


def pack_images(images):
    steps = 8
    return pl.pallas_call(
        pack_images_kernel,
        grid=(steps,),
        in_specs=[
            pl.BlockSpec((128, 1024), lambda t: (0, t)),
            pl.BlockSpec((128, LANES), lambda t: (0, 64 + t)),
        ],
        out_specs=pl.BlockSpec((4, IMG, LANES), lambda t: (t, 0, 0)),
        out_shape=jax.ShapeDtypeStruct((4 * steps, IMG, LANES), F32),
        compiler_params=params(60),
        cost_estimate=cost(0, 9_500_000),
        name="pack_images",
    )(images, images)


def pack_templates_kernel(tpl_ref, bin_ref, class_ref, out_ref):
    bins = jnp.broadcast_to(bin_ref[...].astype(F32), (2, LANES))
    classes = jnp.broadcast_to(class_ref[...].astype(F32), (2, LANES))
    for t in range(8):
        rem = [tpl_ref[b, :, pl.ds((64 + t) * LANES, LANES)] for b in range(4)]
        for q in range(4):
            dest = 4 * t + q
            for j in range(2):
                for b in range(4):
                    out_ref[dest, pl.ds(16 * j + 4 * b, 4), :] = tpl_ref[b, :, pl.ds((2 * dest + j) * LANES, LANES)]
            out_ref[dest, pl.ds(32, 4), :] = pick_groups([turned(rem[b], b - q) for b in range(4)])
            out_ref[dest, pl.ds(META, 2), :] = bins
            out_ref[dest, pl.ds(META + 2, 2), :] = classes


def pack_templates(templates, bins, classes):
    whole = lambda shape: pl.BlockSpec(shape, lambda i: (0,) * len(shape))
    return pl.pallas_call(
        pack_templates_kernel,
        grid=(1,),
        in_specs=[whole(templates.shape), whole((1, LANES)), whole((1, LANES))],
        out_specs=whole((32, TPL, LANES)),
        out_shape=jax.ShapeDtypeStruct((32, TPL, LANES), F32),
        compiler_params=params(60),
        cost_estimate=cost(0, 1_300_000),
        name="pack_templates",
    )(templates, bins, classes)


def operands_kernel(tpl_ref, below_ref, above_ref, ctf_ref, sq_ref, y_ref, ce_ref, tf_ref):
    for block in range(4):
        for d in range(16):
            at = lambda rows: (below_ref, tpl_ref, tpl_ref, above_ref)[block][(d, 2 * d, 2 * d + 1, d)[block], rows, :]
            rows = pl.ds(16 * d, 16)
            tf_ref[rows, pl.ds(0, 128)] = at(pl.ds(0, 16))
            tf_ref[rows, pl.ds(128, 128)] = at(pl.ds(16, 16))
            packed = at(pl.ds(32, 4))
            v = [turned(packed, j) for j in range(4)]
            for b in range(4):
                tail = pick_groups([v[(q - b) % 4] for q in (0, 1, 2)] + [jnp.zeros_like(packed)])
                tf_ref[pl.ds(16 * d + 4 * b, 4), pl.ds(256, 128)] = tail
        for c in range(4):
            out = pl.ds(256 * block + 64 * c, 64)
            full = tf_ref[pl.ds(64 * c, 64), :]
            quad = jnp.dot(full * full, sq_ref[...], precision=HIGHEST, preferred_element_type=F32)
            hi, lo = split(full)
            vh, vl = split(-0.5 * quad)
            lane = lax.broadcasted_iota(jnp.int32, (64, LANES), 1)
            last = jnp.where(lane < 112, vh.astype(F32), vl.astype(F32))
            tail = jnp.where(lane < 64, hi[:, 256:].astype(F32), lo[:, 256:].astype(F32))
            y_ref[out, pl.ds(0, 256)] = hi[:, :256]
            y_ref[out, pl.ds(256, 256)] = lo[:, :256]
            y_ref[out, pl.ds(512, 128)] = jnp.where(lane < 96, tail, last).astype(BF)
    ctf = ctf_ref[...]
    hi, mid = split(ctf)
    ce_ref[pl.ds(0, 16), :] = hi
    ce_ref[pl.ds(16, 16), :] = mid
    ce_ref[pl.ds(32, 16), :] = (ctf - hi.astype(F32) - mid.astype(F32)).astype(BF)


def operands(tpl, below, above, ctf_ext, squares):
    vmem = pl.BlockSpec(memory_space=pltpu.VMEM)
    return pl.pallas_call(
        operands_kernel,
        in_specs=[vmem] * 5,
        out_specs=[vmem, vmem],
        out_shape=[jax.ShapeDtypeStruct((1024, 640), BF), jax.ShapeDtypeStruct((48, 384), BF)],
        scratch_shapes=[pltpu.VMEM((256, 384), F32)],
        compiler_params=params(12),
        cost_estimate=cost(600_000_000, 4_000_000),
        name="operands",
    )(tpl, below, above, ctf_ext, squares)


def bins_of(tpl_ref, sources):
    rows = [tpl_ref[s, pl.ds(META, 1), :] for s in sources]
    return jnp.concatenate(rows, axis=1).astype(jnp.int32)


def scores_kernel(buf0, buf1, buf2, buf3, tpl_ref, y_ref, ce_ref, xh_ref, xl_ref, xr_ref, out_ref):
    step = pl.program_id(0)
    group = lane_group((128, LANES))
    for s, buf_ref in enumerate((buf0, buf1, buf2, buf3)):
        source = 4 * step + s
        classes = tpl_ref[source, pl.ds(META + 2, 1), :].astype(jnp.int32)
        row_class = lax.broadcasted_iota(jnp.int32, (48, 128), 0) % CLASSES
        onehot = jnp.where(row_class == classes, 1.0, 0.0).astype(BF)
        ctf = lax.dot_general(onehot, ce_ref[...], (((0,), (0,)), ((), ())), preferred_element_type=F32)
        for j in range(2):
            hi, lo = split(ctf[:, 128 * j : 128 * j + 128] * buf_ref[0, pl.ds(128 * j, 128), :])
            xh_ref[s, :, pl.ds(128 * j, 128)] = hi
            xl_ref[s, :, pl.ds(128 * j, 128)] = lo
        packed = buf_ref[0, pl.ds(256, 32), :]
        v = [turned(packed, j) for j in range(4)]
        one = jnp.ones_like(packed)
        rem = jnp.concatenate([pick_groups([v[(q - g) % 4] for q in (0, 1, 2)] + [one]) for g in range(4)], axis=0)
        hi, lo = split(ctf[:, 256:] * rem)
        xr_ref[s, :, :] = jnp.where(group == 1, lo.astype(F32), hi.astype(F32)).astype(BF)
    row_bin = lax.broadcasted_iota(jnp.int32, (256, 256), 0) // 4
    for side in range(2):
        pair = (side, 2 + side)
        x = jnp.concatenate(
            [jnp.concatenate([xh_ref[s], xh_ref[s], xl_ref[s], xr_ref[s]], axis=1) for s in pair], axis=0
        )
        mine = row_bin == bins_of(tpl_ref, [4 * step + s for s in pair])
        y = y_ref[pl.ds(256 * side, 768), :]
        y = jnp.concatenate([y[:, :512], y[:, :256], y[:, 512:]], axis=1)
        all_rows = lax.dot_general(y, x, (((1,), (1,)), ((), ())), preferred_element_type=F32)
        for k in range(3):
            kept = jnp.where(mine, all_rows[256 * k : 256 * k + 256], 0.0)
            total = jnp.sum(kept.reshape(32, 8, 256), axis=0)
            total = total + pltpu.roll(total, 4, 0)
            for half, s in enumerate(pair):
                out_ref[3 * s + k] = total[:4, 128 * half : 128 * half + 128]


def window_scores(buf, tpl, y, ctf):
    n = buf.shape[0]
    whole = lambda shape: pl.BlockSpec(shape, lambda p: (0,) * len(shape))
    block = lambda *shape: pl.BlockSpec(shape, lambda p: (p,) + (0,) * (len(shape) - 1))
    image = lambda k: pl.BlockSpec((1, IMG, LANES), lambda p: (4 * p + k, 0, 0))
    return pl.pallas_call(
        scores_kernel,
        grid=(n // 4,),
        in_specs=[image(k) for k in range(4)] + [whole((n, TPL, LANES)), whole((1024, 640)), whole((48, 384))],
        out_specs=[block(4, 128, 256), block(4, 128, 256), block(4, 128, 128), block(12, 4, 128)],
        out_shape=[
            jax.ShapeDtypeStruct((n, 128, 256), BF),
            jax.ShapeDtypeStruct((n, 128, 256), BF),
            jax.ShapeDtypeStruct((n, 128, 128), BF),
            jax.ShapeDtypeStruct((3 * n, 4, 128), F32),
        ],
        compiler_params=params(24),
        cost_estimate=cost(6_000_000_000, 14_000_000),
        name="window_scores",
    )(buf, buf, buf, buf, tpl, y, ctf)


def home_kernel(scores_ref, centre_ref, total_ref, shift_ref, p_ref):
    n = scores_ref.shape[0] // 3
    start = 4 * lax.axis_index("xlo") + 8 * lax.axis_index("z") - 4 - centre_ref[...]
    row = lax.broadcasted_iota(jnp.int32, (4, 128), 0)
    offsets, inside, safe = [], [], []
    for k in range(3):
        scores = scores_ref[k]
        for s in range(1, n):
            scores = scores + scores_ref[3 * s + k]
        offset = row + 4 * k + start
        keep = jnp.abs(offset) <= HALF
        offsets.append(offset.astype(F32))
        inside.append(keep)
        safe.append(jnp.where(keep, scores, 0.0))
    mass = sum(jnp.where(keep, jnp.exp(v), 0.0) for keep, v in zip(inside, safe))
    total = jnp.log(jnp.sum(mass, axis=0, keepdims=True))
    p = [jnp.where(keep, jnp.exp(v - total), 0.0) for keep, v in zip(inside, safe)]
    total_ref[...] = total
    shift_ref[...] = jnp.sum(sum(a * b for a, b in zip(p, offsets)), axis=0, keepdims=True)
    for k in range(3):
        for s in range(n):
            p_ref[3 * s + k] = p[k]


def home(scores, centre):
    vmem = pl.BlockSpec(memory_space=pltpu.VMEM)
    return pl.pallas_call(
        home_kernel,
        in_specs=[vmem, vmem],
        out_specs=[vmem, vmem, vmem],
        out_shape=[
            jax.ShapeDtypeStruct((1, 128), F32),
            jax.ShapeDtypeStruct((1, 128), F32),
            jax.ShapeDtypeStruct(scores.shape, F32),
        ],
        compiler_params=params(4),
        cost_estimate=cost(200_000, 600_000),
        name="home",
    )(scores, centre)


def spread(p8, bins, first_bin, rows):
    n = p8.shape[1]
    row_bin = lax.broadcasted_iota(jnp.int32, (rows, n), 0) // 4 + first_bin
    mine = row_bin == bins
    hi = p8.astype(BF).astype(F32)
    lo = p8 - hi
    wide = lambda v: jnp.broadcast_to(v[None], (rows // 8, 8, n)).reshape(rows, n)
    return [jnp.where(mine, wide(v), 0.0).astype(BF) for v in (hi, lo)]


def sums_kernel(which, p_ref, tpl_ref, xh_ref, xl_ref, xr_ref, out_ref):
    step = pl.program_id(0)

    @pl.when(step == 0)
    def _():
        out_ref[...] = jnp.zeros_like(out_ref)

    def add(rows, parts, sources):
        stack = lambda ref: jnp.concatenate([ref[s] for s in sources], axis=0)
        xh, xl, xr = stack(xh_ref), stack(xl_ref), stack(xr_ref)
        high = jnp.concatenate([part[0] for part in parts], axis=0)
        low = jnp.concatenate([part[1] for part in parts], axis=0)
        left = jnp.concatenate([high, low, high], axis=1)
        main = jnp.dot(left, jnp.concatenate([xh, xh, xl], axis=0), preferred_element_type=F32)
        wide = left.shape[1] // 3 * 2
        tail = jnp.dot(left[:, :wide], jnp.concatenate([xr, xr], axis=0), preferred_element_type=F32)
        out_ref[rows, pl.ds(0, 256)] += main
        out_ref[rows, pl.ds(256, 128)] += tail

    def twice(sources, blocks):
        p4 = jnp.concatenate([p_ref[3 * s + k] for s, k in zip(sources, blocks)], axis=1)
        return jnp.concatenate([p4, p4], axis=0)

    if which == "halo":
        for side in range(2):
            pair = (side, 2 + side)
            bins = bins_of(tpl_ref, [4 * step + s for s in pair])
            p8 = twice(pair, (2 * side, 2 * side))
            add(pl.ds(256 * side, 256), [spread(p8, bins, 0, 256)], pair)
    else:
        four = range(4)
        bins = bins_of(tpl_ref, [4 * step + s for s in four])
        parts = [spread(twice(four, [k + 1 - s % 2 for s in four]), bins, 0, 256) for k in range(2)]
        add(pl.ds(0, 512), parts, four)


def sums(which, p, tpl, xh, xl, xr):
    n = xh.shape[0]
    whole = lambda shape: pl.BlockSpec(shape, lambda i: (0,) * len(shape))
    block = lambda *shape: pl.BlockSpec(shape, lambda i: (i,) + (0,) * (len(shape) - 1))

    def body(*refs):
        sums_kernel(which, *refs)

    return pl.pallas_call(
        body,
        grid=(n // 4,),
        in_specs=[block(12, 4, 128), whole((n, TPL, LANES)), block(4, 128, 256), block(4, 128, 256), block(4, 128, 128)],
        out_specs=whole((512, 384)),
        out_shape=jax.ShapeDtypeStruct((512, 384), F32),
        compiler_params=params(24),
        cost_estimate=cost(4_000_000_000, 6_000_000),
        name="sums_" + which,
    )(p, tpl, xh, xl, xr)


def average_kernel(own_ref, below_ref, above_ref, sq_ref, out_ref):
    for side, other_ref in ((0, below_ref), (1, above_ref)):
        for c in range(4):
            rows = pl.ds(64 * c, 64)
            total = own_ref[pl.ds(256 * side + 64 * c, 64), :] + other_ref[rows, :]
            weight = jnp.dot(total[:, 256:], sq_ref[...], precision=HIGHEST, preferred_element_type=F32)
            tail = total[:, 256:]
            tail = tail + pltpu.roll(tail, 96, 1)
            mean = jnp.concatenate([total[:, :256], tail], axis=1) / (weight + 1.0)
            for d in range(4):
                dest = 2 * (4 * c + d) + side
                rem = []
                for b in range(4):
                    piece = mean[16 * d + 4 * b : 16 * d + 4 * b + 4]
                    out_ref[9 * dest + b] = piece[:, :128]
                    out_ref[9 * dest + 4 + b] = piece[:, 128:256]
                    rem.append(turned(piece[:, 256:], b))
                out_ref[9 * dest + 8] = pick_groups(rem)


def averages(own, below, above, squares, n):
    vmem = pl.BlockSpec(memory_space=pltpu.VMEM)
    return pl.pallas_call(
        average_kernel,
        in_specs=[vmem] * 4,
        out_specs=vmem,
        out_shape=jax.ShapeDtypeStruct((9 * n, 4, LANES), F32),
        compiler_params=params(8),
        cost_estimate=cost(200_000_000, 3_000_000),
        name="averages",
    )(own, below, above, squares)


def unpack_kernel(got_ref, out_ref):
    n = got_ref.shape[0] // 9
    for i in range(n):
        for j in range(2):
            for b in range(4):
                out_ref[b, :, pl.ds(256 * i + 128 * j, 128)] = got_ref[9 * i + 4 * j + b]
    for t in range(n // 4):
        rem = [got_ref[9 * (4 * t + q) + 8] for q in range(4)]
        for b in range(4):
            out_ref[b, :, pl.ds(256 * n + 128 * t, 128)] = pick_groups([turned(rem[q], q - b) for q in range(4)])


def unpack(got, pixels):
    vmem = pl.BlockSpec(memory_space=pltpu.VMEM)
    return pl.pallas_call(
        unpack_kernel,
        in_specs=[vmem],
        out_specs=vmem,
        out_shape=jax.ShapeDtypeStruct((4, 4, pixels), F32),
        compiler_params=params(8),
        cost_estimate=cost(0, 1_200_000),
        name="unpack",
    )(got)


def exchange(value):
    return lax.all_to_all(value, PLANE, split_axis=0, concat_axis=0, tiled=True)


def along_z(value, by):
    size = lax.axis_size("z")
    return lax.ppermute(value, "z", [(i, (i + by) % size) for i in range(size)])


def local(images, prior_bin, prior_center, defocus_class, templates, ctf_table):
    pixels = images.shape[1]
    xlo = lax.axis_index("xlo")
    chunk = lax.axis_index("dir") * 2 + xlo
    ctf_main = lax.dynamic_slice(ctf_table, (0, 256 * chunk), (CLASSES, 256))
    ctf_rem = lax.dynamic_slice(ctf_table, (0, 8192 + 32 * chunk), (CLASSES, 32))
    eye = jnp.eye(CLASSES, dtype=F32)
    ctf_ext = jnp.concatenate([ctf_main, ctf_rem, ctf_rem, ctf_rem, eye, eye], axis=1)
    square = jnp.concatenate([ctf_main, ctf_rem], axis=1)
    square = square * square
    to_class = jnp.pad(jnp.concatenate([square.T, square.T], axis=1), ((0, 96), (96, 0)))
    to_pixel = jnp.pad(square, ((96, 16), (0, 96)))

    tpl = exchange(pack_templates(templates, prior_bin[None], defocus_class[None]))
    n = tpl.shape[0]
    buf = exchange(pack_images(images))
    sides = tpl.reshape(n // 2, 2, TPL, LANES)
    below = along_z(sides[:, 1], 1)
    above = along_z(sides[:, 0], -1)
    y, ctf = operands(tpl, below, above, ctf_ext, to_class)
    xh, xl, xr, partial = window_scores(buf, tpl, y, ctf)
    log_total, mean_shift, p = home(exchange(partial), prior_center[None])
    p = exchange(p)
    edge = sums("halo", p, tpl, xh, xl, xr)
    from_above = along_z(edge[:256], -1)
    from_below = along_z(edge[256:], 1)
    mine = sums("own", p, tpl, xh, xl, xr)
    out = averages(mine, from_below, from_above, to_pixel, n)
    average = unpack(exchange(out), pixels)
    return log_total[0], mean_shift[0], average


def solution(mesh):
    dirs, psis = mesh.devices.shape
    fine = Mesh(mesh.devices.reshape(dirs, psis // 2, 2), ("dir", "z", "xlo"))
    rows = P(("dir", "z", "xlo"))
    grid = P("dir", ("z", "xlo"), None)
    return jax.shard_map(
        local,
        mesh=fine,
        in_specs=(P(("dir", "z", "xlo"), None), rows, rows, rows, grid, P()),
        out_specs=(rows, rows, grid),
        check_vma=False,
    )
```

```python
import jax
import jax.numpy as jnp
from jax import lax
from jax.experimental import pallas as pl
from jax.experimental.pallas import tpu as pltpu
from jax.sharding import Mesh
from jax.sharding import PartitionSpec as P

HALF = 4
LANES = 128
CLASSES = 16
IMG = 288
TPL = 40
META = 36
BF = jnp.bfloat16
F32 = jnp.float32
HIGHEST = lax.Precision.HIGHEST
PLANE = ("dir", "xlo")


def params(mib):
    return pltpu.CompilerParams(vmem_limit_bytes=mib * 1024 * 1024)


def cost(flops, moved):
    return pl.CostEstimate(flops=flops, bytes_accessed=moved, transcendentals=0)


def lane_group(shape):
    return lax.broadcasted_iota(jnp.int32, shape, len(shape) - 1) // 32


def turned(x, groups):
    groups = groups % 4
    return x if groups == 0 else pltpu.roll(x, 32 * groups, x.ndim - 1)


def pick_groups(parts):
    group = lane_group(parts[0].shape)
    out = parts[3]
    for q in (2, 1, 0):
        out = jnp.where(group == q, parts[q], out)
    return out


def split(x):
    hi = x.astype(BF)
    return hi, (x - hi.astype(F32)).astype(BF)


def pack_images_kernel(img_ref, rem_ref, out_ref):
    for q in range(4):
        for j in range(2):
            out_ref[q, pl.ds(j * 128, 128), :] = img_ref[:, pl.ds((2 * q + j) * LANES, LANES)]
        out_ref[q, pl.ds(256, 32), :] = pick_groups([turned(rem_ref[pl.ds(32 * g, 32), :], g - q) for g in range(4)])


def pack_images(images):
    steps = 8
    return pl.pallas_call(
        pack_images_kernel,
        grid=(steps,),
        in_specs=[
            pl.BlockSpec((128, 1024), lambda t: (0, t)),
            pl.BlockSpec((128, LANES), lambda t: (0, 64 + t)),
        ],
        out_specs=pl.BlockSpec((4, IMG, LANES), lambda t: (t, 0, 0)),
        out_shape=jax.ShapeDtypeStruct((4 * steps, IMG, LANES), F32),
        compiler_params=params(60),
        cost_estimate=cost(0, 9_500_000),
        name="pack_images",
    )(images, images)


def pack_templates_kernel(tpl_ref, bin_ref, class_ref, out_ref):
    bins = jnp.broadcast_to(bin_ref[...].astype(F32), (2, LANES))
    classes = jnp.broadcast_to(class_ref[...].astype(F32), (2, LANES))
    for t in range(8):
        rem = [tpl_ref[b, :, pl.ds((64 + t) * LANES, LANES)] for b in range(4)]
        for q in range(4):
            dest = 4 * t + q
            for j in range(2):
                for b in range(4):
                    out_ref[dest, pl.ds(16 * j + 4 * b, 4), :] = tpl_ref[b, :, pl.ds((2 * dest + j) * LANES, LANES)]
            out_ref[dest, pl.ds(32, 4), :] = pick_groups([turned(rem[b], b - q) for b in range(4)])
            out_ref[dest, pl.ds(META, 2), :] = bins
            out_ref[dest, pl.ds(META + 2, 2), :] = classes


def pack_templates(templates, bins, classes):
    whole = lambda shape: pl.BlockSpec(shape, lambda i: (0,) * len(shape))
    return pl.pallas_call(
        pack_templates_kernel,
        grid=(1,),
        in_specs=[whole(templates.shape), whole((1, LANES)), whole((1, LANES))],
        out_specs=whole((32, TPL, LANES)),
        out_shape=jax.ShapeDtypeStruct((32, TPL, LANES), F32),
        compiler_params=params(60),
        cost_estimate=cost(0, 1_300_000),
        name="pack_templates",
    )(templates, bins, classes)


def operands_kernel(tpl_ref, below_ref, above_ref, ctf_ref, sq_ref, y_ref, ce_ref, tf_ref):
    for block in range(4):
        for d in range(16):
            at = lambda rows: (below_ref, tpl_ref, tpl_ref, above_ref)[block][(d, 2 * d, 2 * d + 1, d)[block], rows, :]
            rows = pl.ds(16 * d, 16)
            tf_ref[rows, pl.ds(0, 128)] = at(pl.ds(0, 16))
            tf_ref[rows, pl.ds(128, 128)] = at(pl.ds(16, 16))
            packed = at(pl.ds(32, 4))
            v = [turned(packed, j) for j in range(4)]
            for b in range(4):
                tail = pick_groups([v[(q - b) % 4] for q in (0, 1, 2)] + [jnp.zeros_like(packed)])
                tf_ref[pl.ds(16 * d + 4 * b, 4), pl.ds(256, 128)] = tail
        for c in range(4):
            out = pl.ds(256 * block + 64 * c, 64)
            full = tf_ref[pl.ds(64 * c, 64), :]
            quad = jnp.dot(full * full, sq_ref[...], precision=HIGHEST, preferred_element_type=F32)
            hi, lo = split(full)
            vh, vl = split(-0.5 * quad)
            lane = lax.broadcasted_iota(jnp.int32, (64, LANES), 1)
            last = jnp.where(lane < 112, vh.astype(F32), vl.astype(F32))
            tail = jnp.where(lane < 64, hi[:, 256:].astype(F32), lo[:, 256:].astype(F32))
            y_ref[out, pl.ds(0, 256)] = hi[:, :256]
            y_ref[out, pl.ds(256, 256)] = lo[:, :256]
            y_ref[out, pl.ds(512, 128)] = jnp.where(lane < 96, tail, last).astype(BF)
    ctf = ctf_ref[...]
    hi, mid = split(ctf)
    ce_ref[pl.ds(0, 16), :] = hi
    ce_ref[pl.ds(16, 16), :] = mid
    ce_ref[pl.ds(32, 16), :] = (ctf - hi.astype(F32) - mid.astype(F32)).astype(BF)


def operands(tpl, below, above, ctf_ext, squares):
    vmem = pl.BlockSpec(memory_space=pltpu.VMEM)
    return pl.pallas_call(
        operands_kernel,
        in_specs=[vmem] * 5,
        out_specs=[vmem, vmem],
        out_shape=[jax.ShapeDtypeStruct((1024, 640), BF), jax.ShapeDtypeStruct((48, 384), BF)],
        scratch_shapes=[pltpu.VMEM((256, 384), F32)],
        compiler_params=params(12),
        cost_estimate=cost(600_000_000, 4_000_000),
        name="operands",
    )(tpl, below, above, ctf_ext, squares)


def bins_of(tpl_ref, sources):
    rows = [tpl_ref[s, pl.ds(META, 1), :] for s in sources]
    return jnp.concatenate(rows, axis=1).astype(jnp.int32)


def scores_kernel(buf0, buf1, buf2, buf3, tpl_ref, y_ref, ce_ref, xh_ref, xl_ref, xr_ref, out_ref):
    step = pl.program_id(0)
    group = lane_group((128, LANES))
    for s, buf_ref in enumerate((buf0, buf1, buf2, buf3)):
        source = 4 * step + s
        classes = tpl_ref[source, pl.ds(META + 2, 1), :].astype(jnp.int32)
        row_class = lax.broadcasted_iota(jnp.int32, (48, 128), 0) % CLASSES
        onehot = jnp.where(row_class == classes, 1.0, 0.0).astype(BF)
        ctf = lax.dot_general(onehot, ce_ref[...], (((0,), (0,)), ((), ())), preferred_element_type=F32)
        for j in range(2):
            hi, lo = split(ctf[:, 128 * j : 128 * j + 128] * buf_ref[0, pl.ds(128 * j, 128), :])
            xh_ref[source, :, pl.ds(128 * j, 128)] = hi
            xl_ref[source, :, pl.ds(128 * j, 128)] = lo
        packed = buf_ref[0, pl.ds(256, 32), :]
        v = [turned(packed, j) for j in range(4)]
        one = jnp.ones_like(packed)
        rem = jnp.concatenate([pick_groups([v[(q - g) % 4] for q in (0, 1, 2)] + [one]) for g in range(4)], axis=0)
        hi, lo = split(ctf[:, 256:] * rem)
        xr_ref[source] = jnp.where(group == 1, lo.astype(F32), hi.astype(F32)).astype(BF)
    row_bin = lax.broadcasted_iota(jnp.int32, (256, 256), 0) // 4
    for side in range(2):
        pair = (4 * step + side, 4 * step + 2 + side)
        x = jnp.concatenate(
            [jnp.concatenate([xh_ref[s], xh_ref[s], xl_ref[s], xr_ref[s]], axis=1) for s in pair], axis=0
        )
        mine = row_bin == bins_of(tpl_ref, pair)
        y = y_ref[pl.ds(256 * side, 768), :]
        y = jnp.concatenate([y[:, :512], y[:, :256], y[:, 512:]], axis=1)
        all_rows = lax.dot_general(y, x, (((1,), (1,)), ((), ())), preferred_element_type=F32)
        for k in range(3):
            kept = jnp.where(mine, all_rows[256 * k : 256 * k + 256], 0.0)
            total = jnp.sum(kept.reshape(32, 8, 256), axis=0)
            total = total + pltpu.roll(total, 4, 0)
            for half, s in enumerate(pair):
                out_ref[3 * s + k] = total[:4, 128 * half : 128 * half + 128]


def window_scores(buf, tpl, y, ctf):
    n = buf.shape[0]
    vmem = pl.BlockSpec(memory_space=pltpu.VMEM)
    image = lambda k: pl.BlockSpec((1, IMG, LANES), lambda p: (4 * p + k, 0, 0))
    return pl.pallas_call(
        scores_kernel,
        grid=(n // 4,),
        in_specs=[image(k) for k in range(4)] + [vmem] * 3,
        out_specs=[vmem] * 4,
        out_shape=[
            jax.ShapeDtypeStruct((n, 128, 256), BF),
            jax.ShapeDtypeStruct((n, 128, 256), BF),
            jax.ShapeDtypeStruct((n, 128, 128), BF),
            jax.ShapeDtypeStruct((3 * n, 4, 128), F32),
        ],
        compiler_params=params(24),
        cost_estimate=cost(6_000_000_000, 14_000_000),
        name="window_scores",
    )(buf, buf, buf, buf, tpl, y, ctf)


def home_kernel(scores_ref, centre_ref, total_ref, shift_ref, p_ref):
    n = scores_ref.shape[0] // 3
    start = 4 * lax.axis_index("xlo") + 8 * lax.axis_index("z") - 4 - centre_ref[...]
    row = lax.broadcasted_iota(jnp.int32, (4, 128), 0)
    offsets, inside, safe = [], [], []
    for k in range(3):
        scores = scores_ref[k]
        for s in range(1, n):
            scores = scores + scores_ref[3 * s + k]
        offset = row + 4 * k + start
        keep = jnp.abs(offset) <= HALF
        offsets.append(offset.astype(F32))
        inside.append(keep)
        safe.append(jnp.where(keep, scores, 0.0))
    mass = sum(jnp.where(keep, jnp.exp(v), 0.0) for keep, v in zip(inside, safe))
    total = jnp.log(jnp.sum(mass, axis=0, keepdims=True))
    p = [jnp.where(keep, jnp.exp(v - total), 0.0) for keep, v in zip(inside, safe)]
    total_ref[...] = total
    shift_ref[...] = jnp.sum(sum(a * b for a, b in zip(p, offsets)), axis=0, keepdims=True)
    for k in range(3):
        for s in range(n):
            p_ref[3 * s + k] = p[k]


def home(scores, centre):
    vmem = pl.BlockSpec(memory_space=pltpu.VMEM)
    return pl.pallas_call(
        home_kernel,
        in_specs=[vmem, vmem],
        out_specs=[vmem, vmem, vmem],
        out_shape=[
            jax.ShapeDtypeStruct((1, 128), F32),
            jax.ShapeDtypeStruct((1, 128), F32),
            jax.ShapeDtypeStruct(scores.shape, F32),
        ],
        compiler_params=params(4),
        cost_estimate=cost(200_000, 600_000),
        name="home",
    )(scores, centre)


def spread(p8, bins, first_bin, rows):
    n = p8.shape[1]
    row_bin = lax.broadcasted_iota(jnp.int32, (rows, n), 0) // 4 + first_bin
    mine = row_bin == bins
    hi = p8.astype(BF).astype(F32)
    lo = p8 - hi
    wide = lambda v: jnp.broadcast_to(v[None], (rows // 8, 8, n)).reshape(rows, n)
    return [jnp.where(mine, wide(v), 0.0).astype(BF) for v in (hi, lo)]


def sums_kernel(which, p_ref, tpl_ref, xh_ref, xl_ref, xr_ref, out_ref):
    step = pl.program_id(0)

    @pl.when(step == 0)
    def _():
        out_ref[...] = jnp.zeros_like(out_ref)

    def add(rows, parts, sources):
        stack = lambda ref: jnp.concatenate([ref[s] for s in sources], axis=0)
        xh, xl, xr = stack(xh_ref), stack(xl_ref), stack(xr_ref)
        high = jnp.concatenate([part[0] for part in parts], axis=0)
        low = jnp.concatenate([part[1] for part in parts], axis=0)
        left = jnp.concatenate([high, low, high], axis=1)
        main = jnp.dot(left, jnp.concatenate([xh, xh, xl], axis=0), preferred_element_type=F32)
        wide = left.shape[1] // 3 * 2
        tail = jnp.dot(left[:, :wide], jnp.concatenate([xr, xr], axis=0), preferred_element_type=F32)
        out_ref[rows, pl.ds(0, 256)] += main
        out_ref[rows, pl.ds(256, 128)] += tail

    def twice(sources, blocks):
        p4 = jnp.concatenate([p_ref[3 * s + k] for s, k in zip(sources, blocks)], axis=1)
        return jnp.concatenate([p4, p4], axis=0)

    if which == "halo":
        for side in range(2):
            pair = (4 * step + side, 4 * step + 2 + side)
            bins = bins_of(tpl_ref, pair)
            p8 = twice(pair, (2 * side, 2 * side))
            add(pl.ds(256 * side, 256), [spread(p8, bins, 0, 256)], pair)
    else:
        four = [4 * step + s for s in range(4)]
        bins = bins_of(tpl_ref, four)
        parts = [spread(twice(four, [k + 1, k, k + 1, k]), bins, 0, 256) for k in range(2)]
        add(pl.ds(0, 512), parts, four)


def sums(which, p, tpl, xh, xl, xr):
    n = xh.shape[0]
    vmem = pl.BlockSpec(memory_space=pltpu.VMEM)

    def body(*refs):
        sums_kernel(which, *refs)

    return pl.pallas_call(
        body,
        grid=(n // 4,),
        in_specs=[vmem] * 5,
        out_specs=vmem,
        out_shape=jax.ShapeDtypeStruct((512, 384), F32),
        compiler_params=params(24),
        cost_estimate=cost(4_000_000_000, 6_000_000),
        name="sums_" + which,
    )(p, tpl, xh, xl, xr)


def average_kernel(own_ref, below_ref, above_ref, sq_ref, out_ref):
    for side, other_ref in ((0, below_ref), (1, above_ref)):
        for c in range(4):
            rows = pl.ds(64 * c, 64)
            total = own_ref[pl.ds(256 * side + 64 * c, 64), :] + other_ref[rows, :]
            weight = jnp.dot(total[:, 256:], sq_ref[...], precision=HIGHEST, preferred_element_type=F32)
            tail = total[:, 256:]
            tail = tail + pltpu.roll(tail, 96, 1)
            mean = jnp.concatenate([total[:, :256], tail], axis=1) / (weight + 1.0)
            for d in range(4):
                dest = 2 * (4 * c + d) + side
                rem = []
                for b in range(4):
                    piece = mean[16 * d + 4 * b : 16 * d + 4 * b + 4]
                    out_ref[9 * dest + b] = piece[:, :128]
                    out_ref[9 * dest + 4 + b] = piece[:, 128:256]
                    rem.append(turned(piece[:, 256:], b))
                out_ref[9 * dest + 8] = pick_groups(rem)


def averages(own, below, above, squares, n):
    vmem = pl.BlockSpec(memory_space=pltpu.VMEM)
    return pl.pallas_call(
        average_kernel,
        in_specs=[vmem] * 4,
        out_specs=vmem,
        out_shape=jax.ShapeDtypeStruct((9 * n, 4, LANES), F32),
        compiler_params=params(8),
        cost_estimate=cost(200_000_000, 3_000_000),
        name="averages",
    )(own, below, above, squares)


def unpack_kernel(got_ref, out_ref):
    n = got_ref.shape[0] // 9
    for i in range(n):
        for j in range(2):
            for b in range(4):
                out_ref[b, :, pl.ds(256 * i + 128 * j, 128)] = got_ref[9 * i + 4 * j + b]
    for t in range(n // 4):
        rem = [got_ref[9 * (4 * t + q) + 8] for q in range(4)]
        for b in range(4):
            out_ref[b, :, pl.ds(256 * n + 128 * t, 128)] = pick_groups([turned(rem[q], q - b) for q in range(4)])


def unpack(got, pixels):
    vmem = pl.BlockSpec(memory_space=pltpu.VMEM)
    return pl.pallas_call(
        unpack_kernel,
        in_specs=[vmem],
        out_specs=vmem,
        out_shape=jax.ShapeDtypeStruct((4, 4, pixels), F32),
        compiler_params=params(8),
        cost_estimate=cost(0, 1_200_000),
        name="unpack",
    )(got)


def exchange(value):
    return lax.all_to_all(value, PLANE, split_axis=0, concat_axis=0, tiled=True)


def along_z(value, by):
    size = lax.axis_size("z")
    return lax.ppermute(value, "z", [(i, (i + by) % size) for i in range(size)])


def local(images, prior_bin, prior_center, defocus_class, templates, ctf_table):
    pixels = images.shape[1]
    xlo = lax.axis_index("xlo")
    chunk = lax.axis_index("dir") * 2 + xlo
    ctf_main = lax.dynamic_slice(ctf_table, (0, 256 * chunk), (CLASSES, 256))
    ctf_rem = lax.dynamic_slice(ctf_table, (0, 8192 + 32 * chunk), (CLASSES, 32))
    eye = jnp.eye(CLASSES, dtype=F32)
    ctf_ext = jnp.concatenate([ctf_main, ctf_rem, ctf_rem, ctf_rem, eye, eye], axis=1)
    square = jnp.concatenate([ctf_main, ctf_rem], axis=1)
    square = square * square
    to_class = jnp.pad(jnp.concatenate([square.T, square.T], axis=1), ((0, 96), (96, 0)))
    to_pixel = jnp.pad(square, ((96, 16), (0, 96)))

    tpl = exchange(pack_templates(templates, prior_bin[None], defocus_class[None]))
    n = tpl.shape[0]
    buf = exchange(pack_images(images))
    sides = tpl.reshape(n // 2, 2, TPL, LANES)
    below = along_z(sides[:, 1], 1)
    above = along_z(sides[:, 0], -1)
    y, ctf = operands(tpl, below, above, ctf_ext, to_class)
    xh, xl, xr, partial = window_scores(buf, tpl, y, ctf)
    log_total, mean_shift, p = home(exchange(partial), prior_center[None])
    p = exchange(p)
    edge = sums("halo", p, tpl, xh, xl, xr)
    from_above = along_z(edge[:256], -1)
    from_below = along_z(edge[256:], 1)
    mine = sums("own", p, tpl, xh, xl, xr)
    out = averages(mine, from_below, from_above, to_pixel, n)
    average = unpack(exchange(out), pixels)
    return log_total[0], mean_shift[0], average


def solution(mesh):
    dirs, psis = mesh.devices.shape
    fine = Mesh(mesh.devices.reshape(dirs, psis // 2, 2), ("dir", "z", "xlo"))
    rows = P(("dir", "z", "xlo"))
    grid = P("dir", ("z", "xlo"), None)
    return jax.shard_map(
        local,
        mesh=fine,
        in_specs=(P(("dir", "z", "xlo"), None), rows, rows, rows, grid, P()),
        out_specs=(rows, rows, grid),
        check_vma=False,
    )
```

```python
import jax
import jax.numpy as jnp
from jax import lax
from jax.experimental import pallas as pl
from jax.experimental.pallas import tpu as pltpu
from jax.sharding import Mesh
from jax.sharding import PartitionSpec as P

HALF = 4
LANES = 128
CLASSES = 16
IMG = 288
TPL = 40
META = 36
BF = jnp.bfloat16
F32 = jnp.float32
HIGHEST = lax.Precision.HIGHEST
PLANE = ("dir", "xlo")


def params(mib):
    return pltpu.CompilerParams(vmem_limit_bytes=mib * 1024 * 1024)


def cost(flops, moved):
    return pl.CostEstimate(flops=flops, bytes_accessed=moved, transcendentals=0)


def lane_group(shape):
    return lax.broadcasted_iota(jnp.int32, shape, len(shape) - 1) // 32


def turned(x, groups):
    groups = groups % 4
    return x if groups == 0 else pltpu.roll(x, 32 * groups, x.ndim - 1)


def pick_groups(parts):
    group = lane_group(parts[0].shape)
    out = parts[3]
    for q in (2, 1, 0):
        out = jnp.where(group == q, parts[q], out)
    return out


def split(x):
    hi = x.astype(BF)
    return hi, (x - hi.astype(F32)).astype(BF)


def pack_images_kernel(img_ref, rem_ref, out_ref):
    for q in range(4):
        for j in range(2):
            out_ref[q, pl.ds(j * 128, 128), :] = img_ref[:, pl.ds((2 * q + j) * LANES, LANES)]
        out_ref[q, pl.ds(256, 32), :] = pick_groups([turned(rem_ref[pl.ds(32 * g, 32), :], g - q) for g in range(4)])


def pack_images(images):
    steps = 8
    return pl.pallas_call(
        pack_images_kernel,
        grid=(steps,),
        in_specs=[
            pl.BlockSpec((128, 1024), lambda t: (0, t)),
            pl.BlockSpec((128, LANES), lambda t: (0, 64 + t)),
        ],
        out_specs=pl.BlockSpec((4, IMG, LANES), lambda t: (t, 0, 0)),
        out_shape=jax.ShapeDtypeStruct((4 * steps, IMG, LANES), F32),
        compiler_params=params(60),
        cost_estimate=cost(0, 9_500_000),
        name="pack_images",
    )(images, images)


def pack_templates_kernel(tpl_ref, bin_ref, class_ref, out_ref):
    bins = jnp.broadcast_to(bin_ref[...].astype(F32), (2, LANES))
    classes = jnp.broadcast_to(class_ref[...].astype(F32), (2, LANES))
    for t in range(8):
        rem = [tpl_ref[b, :, pl.ds((64 + t) * LANES, LANES)] for b in range(4)]
        for q in range(4):
            dest = 4 * t + q
            for j in range(2):
                for b in range(4):
                    out_ref[dest, pl.ds(16 * j + 4 * b, 4), :] = tpl_ref[b, :, pl.ds((2 * dest + j) * LANES, LANES)]
            out_ref[dest, pl.ds(32, 4), :] = pick_groups([turned(rem[b], b - q) for b in range(4)])
            out_ref[dest, pl.ds(META, 2), :] = bins
            out_ref[dest, pl.ds(META + 2, 2), :] = classes


def pack_templates(templates, bins, classes):
    whole = lambda shape: pl.BlockSpec(shape, lambda i: (0,) * len(shape))
    return pl.pallas_call(
        pack_templates_kernel,
        grid=(1,),
        in_specs=[whole(templates.shape), whole((1, LANES)), whole((1, LANES))],
        out_specs=whole((32, TPL, LANES)),
        out_shape=jax.ShapeDtypeStruct((32, TPL, LANES), F32),
        compiler_params=params(60),
        cost_estimate=cost(0, 1_300_000),
        name="pack_templates",
    )(templates, bins, classes)


def operands_kernel(tpl_ref, below_ref, above_ref, ctf_ref, sq_ref, y_ref, ce_ref, tf_ref):
    for block in range(4):
        for d in range(16):
            at = lambda rows: (below_ref, tpl_ref, tpl_ref, above_ref)[block][(d, 2 * d, 2 * d + 1, d)[block], rows, :]
            rows = pl.ds(16 * d, 16)
            tf_ref[rows, pl.ds(0, 128)] = at(pl.ds(0, 16))
            tf_ref[rows, pl.ds(128, 128)] = at(pl.ds(16, 16))
            packed = at(pl.ds(32, 4))
            v = [turned(packed, j) for j in range(4)]
            for b in range(4):
                tail = pick_groups([v[(q - b) % 4] for q in (0, 1, 2)] + [jnp.zeros_like(packed)])
                tf_ref[pl.ds(16 * d + 4 * b, 4), pl.ds(256, 128)] = tail
        for c in range(4):
            out = pl.ds(256 * block + 64 * c, 64)
            full = tf_ref[pl.ds(64 * c, 64), :]
            quad = jnp.dot(full * full, sq_ref[...], precision=HIGHEST, preferred_element_type=F32)
            hi, lo = split(full)
            vh, vl = split(-0.5 * quad)
            lane = lax.broadcasted_iota(jnp.int32, (64, LANES), 1)
            last = jnp.where(lane < 112, vh.astype(F32), vl.astype(F32))
            tail = jnp.where(lane < 64, hi[:, 256:].astype(F32), lo[:, 256:].astype(F32))
            y_ref[out, pl.ds(0, 256)] = hi[:, :256]
            y_ref[out, pl.ds(256, 256)] = lo[:, :256]
            y_ref[out, pl.ds(512, 128)] = jnp.where(lane < 96, tail, last).astype(BF)
    ctf = ctf_ref[...]
    hi, mid = split(ctf)
    ce_ref[pl.ds(0, 16), :] = hi
    ce_ref[pl.ds(16, 16), :] = mid
    ce_ref[pl.ds(32, 16), :] = (ctf - hi.astype(F32) - mid.astype(F32)).astype(BF)


def operands(tpl, below, above, ctf_ext, squares):
    vmem = pl.BlockSpec(memory_space=pltpu.VMEM)
    return pl.pallas_call(
        operands_kernel,
        in_specs=[vmem] * 5,
        out_specs=[vmem, vmem],
        out_shape=[jax.ShapeDtypeStruct((1024, 640), BF), jax.ShapeDtypeStruct((48, 384), BF)],
        scratch_shapes=[pltpu.VMEM((256, 384), F32)],
        compiler_params=params(12),
        cost_estimate=cost(600_000_000, 4_000_000),
        name="operands",
    )(tpl, below, above, ctf_ext, squares)


def bins_of(tpl_ref, sources):
    rows = [tpl_ref[s, pl.ds(META, 1), :] for s in sources]
    return jnp.concatenate(rows, axis=1).astype(jnp.int32)


def weigh(buf_ref, step, tpl_ref, ce_ref, x_ref, xh_ref, xl_ref, xr_ref):
    group = lane_group((128, LANES))
    for s in range(4):
        source = 4 * step + s
        classes = tpl_ref[source, pl.ds(META + 2, 1), :].astype(jnp.int32)
        row_class = lax.broadcasted_iota(jnp.int32, (48, 128), 0) % CLASSES
        onehot = jnp.where(row_class == classes, 1.0, 0.0).astype(BF)
        ctf = lax.dot_general(onehot, ce_ref[...], (((0,), (0,)), ((), ())), preferred_element_type=F32)
        rows = pl.ds(256 * (s % 2) + 128 * (s // 2), 128)
        for j in range(2):
            hi, lo = split(ctf[:, 128 * j : 128 * j + 128] * buf_ref[s, pl.ds(128 * j, 128), :])
            xh_ref[source, :, pl.ds(128 * j, 128)] = hi
            xl_ref[source, :, pl.ds(128 * j, 128)] = lo
            x_ref[rows, pl.ds(128 * j, 128)] = hi
            x_ref[rows, pl.ds(256 + 128 * j, 128)] = lo
        packed = buf_ref[s, pl.ds(256, 32), :]
        v = [turned(packed, j) for j in range(4)]
        one = jnp.ones_like(packed)
        rem = jnp.concatenate([pick_groups([v[(q - g) % 4] for q in (0, 1, 2)] + [one]) for g in range(4)], axis=0)
        hi, lo = split(ctf[:, 256:] * rem)
        tail = jnp.where(group == 1, lo.astype(F32), hi.astype(F32)).astype(BF)
        xr_ref[source] = tail
        x_ref[rows, pl.ds(512, 128)] = tail


def score(step, x_ref, tpl_ref, y_ref, out_ref):
    row_bin = lax.broadcasted_iota(jnp.int32, (256, 256), 0) // 4
    for side in range(2):
        pair = (4 * step + side, 4 * step + 2 + side)
        x = x_ref[pl.ds(256 * side, 256), :]
        x = jnp.concatenate([x[:, :256], x], axis=1)
        mine = row_bin == bins_of(tpl_ref, pair)
        y = y_ref[pl.ds(256 * side, 768), :]
        y = jnp.concatenate([y[:, :512], y[:, :256], y[:, 512:]], axis=1)
        all_rows = lax.dot_general(y, x, (((1,), (1,)), ((), ())), preferred_element_type=F32)
        for k in range(3):
            kept = jnp.where(mine, all_rows[256 * k : 256 * k + 256], 0.0)
            total = jnp.sum(kept.reshape(32, 8, 256), axis=0)
            total = total + pltpu.roll(total, 4, 0)
            for half, s in enumerate(pair):
                out_ref[3 * s + k] = total[:4, 128 * half : 128 * half + 128]


def scores_kernel(first_ref, odd_ref, even_ref, tpl_ref, y_ref, ce_ref, xh_ref, xl_ref, xr_ref, out_ref, xa_ref, xb_ref):
    i = pl.program_id(0)
    last = 2 * pl.num_programs(0) - 1
    kept = (xh_ref, xl_ref, xr_ref)

    @pl.when(i == 0)
    def _():
        weigh(first_ref, 0, tpl_ref, ce_ref, xa_ref, *kept)

    weigh(odd_ref, 2 * i + 1, tpl_ref, ce_ref, xb_ref, *kept)
    score(2 * i, xa_ref, tpl_ref, y_ref, out_ref)
    weigh(even_ref, jnp.minimum(2 * i + 2, last), tpl_ref, ce_ref, xa_ref, *kept)
    score(2 * i + 1, xb_ref, tpl_ref, y_ref, out_ref)


def window_scores(buf, tpl, y, ctf):
    n = buf.shape[0]
    blocks = n // 4
    vmem = pl.BlockSpec(memory_space=pltpu.VMEM)
    image = lambda at: pl.BlockSpec((4, IMG, LANES), lambda p: (at(p), 0, 0))
    return pl.pallas_call(
        scores_kernel,
        grid=(blocks // 2,),
        in_specs=[image(lambda p: 0), image(lambda p: 2 * p + 1), image(lambda p: jnp.minimum(2 * p + 2, blocks - 1))] + [vmem] * 3,
        out_specs=[vmem] * 4,
        out_shape=[
            jax.ShapeDtypeStruct((n, 128, 256), BF),
            jax.ShapeDtypeStruct((n, 128, 256), BF),
            jax.ShapeDtypeStruct((n, 128, 128), BF),
            jax.ShapeDtypeStruct((3 * n, 4, 128), F32),
        ],
        scratch_shapes=[pltpu.VMEM((512, 640), BF), pltpu.VMEM((512, 640), BF)],
        compiler_params=params(24),
        cost_estimate=cost(6_000_000_000, 14_000_000),
        name="window_scores",
    )(buf, buf, buf, tpl, y, ctf)


def home_kernel(scores_ref, centre_ref, total_ref, shift_ref, p_ref):
    n = scores_ref.shape[0] // 3
    start = 4 * lax.axis_index("xlo") + 8 * lax.axis_index("z") - 4 - centre_ref[...]
    row = lax.broadcasted_iota(jnp.int32, (4, 128), 0)
    offsets, inside, safe = [], [], []
    for k in range(3):
        scores = scores_ref[k]
        for s in range(1, n):
            scores = scores + scores_ref[3 * s + k]
        offset = row + 4 * k + start
        keep = jnp.abs(offset) <= HALF
        offsets.append(offset.astype(F32))
        inside.append(keep)
        safe.append(jnp.where(keep, scores, 0.0))
    mass = sum(jnp.where(keep, jnp.exp(v), 0.0) for keep, v in zip(inside, safe))
    total = jnp.log(jnp.sum(mass, axis=0, keepdims=True))
    p = [jnp.where(keep, jnp.exp(v - total), 0.0) for keep, v in zip(inside, safe)]
    total_ref[...] = total
    shift_ref[...] = jnp.sum(sum(a * b for a, b in zip(p, offsets)), axis=0, keepdims=True)
    for k in range(3):
        for s in range(n):
            p_ref[3 * s + k] = p[k]


def home(scores, centre):
    vmem = pl.BlockSpec(memory_space=pltpu.VMEM)
    return pl.pallas_call(
        home_kernel,
        in_specs=[vmem, vmem],
        out_specs=[vmem, vmem, vmem],
        out_shape=[
            jax.ShapeDtypeStruct((1, 128), F32),
            jax.ShapeDtypeStruct((1, 128), F32),
            jax.ShapeDtypeStruct(scores.shape, F32),
        ],
        compiler_params=params(4),
        cost_estimate=cost(200_000, 600_000),
        name="home",
    )(scores, centre)


def spread(p8, bins, first_bin, rows):
    n = p8.shape[1]
    row_bin = lax.broadcasted_iota(jnp.int32, (rows, n), 0) // 4 + first_bin
    mine = row_bin == bins
    hi = p8.astype(BF).astype(F32)
    lo = p8 - hi
    wide = lambda v: jnp.broadcast_to(v[None], (rows // 8, 8, n)).reshape(rows, n)
    return [jnp.where(mine, wide(v), 0.0).astype(BF) for v in (hi, lo)]


def sums_kernel(which, p_ref, tpl_ref, xh_ref, xl_ref, xr_ref, out_ref):
    step = pl.program_id(0)

    @pl.when(step == 0)
    def _():
        out_ref[...] = jnp.zeros_like(out_ref)

    def add(rows, parts, sources):
        stack = lambda ref: jnp.concatenate([ref[s] for s in sources], axis=0)
        xh, xl, xr = stack(xh_ref), stack(xl_ref), stack(xr_ref)
        high = jnp.concatenate([part[0] for part in parts], axis=0)
        low = jnp.concatenate([part[1] for part in parts], axis=0)
        left = jnp.concatenate([high, low, high], axis=1)
        main = jnp.dot(left, jnp.concatenate([xh, xh, xl], axis=0), preferred_element_type=F32)
        wide = left.shape[1] // 3 * 2
        tail = jnp.dot(left[:, :wide], jnp.concatenate([xr, xr], axis=0), preferred_element_type=F32)
        out_ref[rows, pl.ds(0, 256)] += main
        out_ref[rows, pl.ds(256, 128)] += tail

    def twice(sources, blocks):
        p4 = jnp.concatenate([p_ref[3 * s + k] for s, k in zip(sources, blocks)], axis=1)
        return jnp.concatenate([p4, p4], axis=0)

    if which == "halo":
        for side in range(2):
            pair = (4 * step + side, 4 * step + 2 + side)
            bins = bins_of(tpl_ref, pair)
            p8 = twice(pair, (2 * side, 2 * side))
            add(pl.ds(256 * side, 256), [spread(p8, bins, 0, 256)], pair)
    else:
        four = [4 * step + s for s in range(4)]
        bins = bins_of(tpl_ref, four)
        parts = [spread(twice(four, [k + 1, k, k + 1, k]), bins, 0, 256) for k in range(2)]
        add(pl.ds(0, 512), parts, four)


def sums(which, p, tpl, xh, xl, xr):
    n = xh.shape[0]
    vmem = pl.BlockSpec(memory_space=pltpu.VMEM)

    def body(*refs):
        sums_kernel(which, *refs)

    return pl.pallas_call(
        body,
        grid=(n // 4,),
        in_specs=[vmem] * 5,
        out_specs=vmem,
        out_shape=jax.ShapeDtypeStruct((512, 384), F32),
        compiler_params=params(24),
        cost_estimate=cost(4_000_000_000, 6_000_000),
        name="sums_" + which,
    )(p, tpl, xh, xl, xr)


def average_kernel(own_ref, below_ref, above_ref, sq_ref, out_ref):
    for side, other_ref in ((0, below_ref), (1, above_ref)):
        for c in range(4):
            rows = pl.ds(64 * c, 64)
            total = own_ref[pl.ds(256 * side + 64 * c, 64), :] + other_ref[rows, :]
            weight = jnp.dot(total[:, 256:], sq_ref[...], precision=HIGHEST, preferred_element_type=F32)
            tail = total[:, 256:]
            tail = tail + pltpu.roll(tail, 96, 1)
            mean = jnp.concatenate([total[:, :256], tail], axis=1) / (weight + 1.0)
            for d in range(4):
                dest = 2 * (4 * c + d) + side
                rem = []
                for b in range(4):
                    piece = mean[16 * d + 4 * b : 16 * d + 4 * b + 4]
                    out_ref[9 * dest + b] = piece[:, :128]
                    out_ref[9 * dest + 4 + b] = piece[:, 128:256]
                    rem.append(turned(piece[:, 256:], b))
                out_ref[9 * dest + 8] = pick_groups(rem)


def averages(own, below, above, squares, n):
    vmem = pl.BlockSpec(memory_space=pltpu.VMEM)
    return pl.pallas_call(
        average_kernel,
        in_specs=[vmem] * 4,
        out_specs=vmem,
        out_shape=jax.ShapeDtypeStruct((9 * n, 4, LANES), F32),
        compiler_params=params(8),
        cost_estimate=cost(200_000_000, 3_000_000),
        name="averages",
    )(own, below, above, squares)


def unpack_kernel(got_ref, out_ref):
    n = got_ref.shape[0] // 9
    for i in range(n):
        for j in range(2):
            for b in range(4):
                out_ref[b, :, pl.ds(256 * i + 128 * j, 128)] = got_ref[9 * i + 4 * j + b]
    for t in range(n // 4):
        rem = [got_ref[9 * (4 * t + q) + 8] for q in range(4)]
        for b in range(4):
            out_ref[b, :, pl.ds(256 * n + 128 * t, 128)] = pick_groups([turned(rem[q], q - b) for q in range(4)])


def unpack(got, pixels):
    vmem = pl.BlockSpec(memory_space=pltpu.VMEM)
    return pl.pallas_call(
        unpack_kernel,
        in_specs=[vmem],
        out_specs=vmem,
        out_shape=jax.ShapeDtypeStruct((4, 4, pixels), F32),
        compiler_params=params(8),
        cost_estimate=cost(0, 1_200_000),
        name="unpack",
    )(got)


def exchange(value):
    return lax.all_to_all(value, PLANE, split_axis=0, concat_axis=0, tiled=True)


def along_z(value, by):
    size = lax.axis_size("z")
    return lax.ppermute(value, "z", [(i, (i + by) % size) for i in range(size)])


def local(images, prior_bin, prior_center, defocus_class, templates, ctf_table):
    pixels = images.shape[1]
    xlo = lax.axis_index("xlo")
    chunk = lax.axis_index("dir") * 2 + xlo
    ctf_main = lax.dynamic_slice(ctf_table, (0, 256 * chunk), (CLASSES, 256))
    ctf_rem = lax.dynamic_slice(ctf_table, (0, 8192 + 32 * chunk), (CLASSES, 32))
    eye = jnp.eye(CLASSES, dtype=F32)
    ctf_ext = jnp.concatenate([ctf_main, ctf_rem, ctf_rem, ctf_rem, eye, eye], axis=1)
    square = jnp.concatenate([ctf_main, ctf_rem], axis=1)
    square = square * square
    to_class = jnp.pad(jnp.concatenate([square.T, square.T], axis=1), ((0, 96), (96, 0)))
    to_pixel = jnp.pad(square, ((96, 16), (0, 96)))

    tpl = exchange(pack_templates(templates, prior_bin[None], defocus_class[None]))
    n = tpl.shape[0]
    buf = exchange(pack_images(images))
    sides = tpl.reshape(n // 2, 2, TPL, LANES)
    below = along_z(sides[:, 1], 1)
    above = along_z(sides[:, 0], -1)
    y, ctf = operands(tpl, below, above, ctf_ext, to_class)
    xh, xl, xr, partial = window_scores(buf, tpl, y, ctf)
    log_total, mean_shift, p = home(exchange(partial), prior_center[None])
    p = exchange(p)
    edge = sums("halo", p, tpl, xh, xl, xr)
    from_above = along_z(edge[:256], -1)
    from_below = along_z(edge[256:], 1)
    mine = sums("own", p, tpl, xh, xl, xr)
    out = averages(mine, from_below, from_above, to_pixel, n)
    average = unpack(exchange(out), pixels)
    return log_total[0], mean_shift[0], average


def solution(mesh):
    dirs, psis = mesh.devices.shape
    fine = Mesh(mesh.devices.reshape(dirs, psis // 2, 2), ("dir", "z", "xlo"))
    rows = P(("dir", "z", "xlo"))
    grid = P("dir", ("z", "xlo"), None)
    return jax.shard_map(
        local,
        mesh=fine,
        in_specs=(P(("dir", "z", "xlo"), None), rows, rows, rows, grid, P()),
        out_specs=(rows, rows, grid),
        check_vma=False,
    )
```

```python
import jax
import jax.numpy as jnp
from jax import lax
from jax.experimental import pallas as pl
from jax.experimental.pallas import tpu as pltpu
from jax.sharding import Mesh
from jax.sharding import PartitionSpec as P

HALF = 4
LANES = 128
CLASSES = 16
IMG = 288
TPL = 40
META = 36
BF = jnp.bfloat16
F32 = jnp.float32
HIGHEST = lax.Precision.HIGHEST
PLANE = ("dir", "xlo")


def params(mib):
    return pltpu.CompilerParams(vmem_limit_bytes=mib * 1024 * 1024)


def cost(flops, moved):
    return pl.CostEstimate(flops=flops, bytes_accessed=moved, transcendentals=0)


def lane_group(shape):
    return lax.broadcasted_iota(jnp.int32, shape, len(shape) - 1) // 32


def turned(x, groups):
    groups = groups % 4
    return x if groups == 0 else pltpu.roll(x, 32 * groups, x.ndim - 1)


def pick_groups(parts):
    group = lane_group(parts[0].shape)
    out = parts[3]
    for q in (2, 1, 0):
        out = jnp.where(group == q, parts[q], out)
    return out


def split(x):
    hi = x.astype(BF)
    return hi, (x - hi.astype(F32)).astype(BF)


def pack_images_kernel(img_ref, rem_ref, out_ref):
    for q in range(4):
        for j in range(2):
            out_ref[q, pl.ds(j * 128, 128), :] = img_ref[:, pl.ds((2 * q + j) * LANES, LANES)]
        out_ref[q, pl.ds(256, 32), :] = pick_groups([turned(rem_ref[pl.ds(32 * g, 32), :], g - q) for g in range(4)])


def pack_images(images):
    steps = 8
    return pl.pallas_call(
        pack_images_kernel,
        grid=(steps,),
        in_specs=[
            pl.BlockSpec((128, 1024), lambda t: (0, t)),
            pl.BlockSpec((128, LANES), lambda t: (0, 64 + t)),
        ],
        out_specs=pl.BlockSpec((4, IMG, LANES), lambda t: (t, 0, 0)),
        out_shape=jax.ShapeDtypeStruct((4 * steps, IMG, LANES), F32),
        compiler_params=params(60),
        cost_estimate=cost(0, 9_500_000),
        name="pack_images",
    )(images, images)


def pack_templates_kernel(tpl_ref, bin_ref, class_ref, out_ref):
    bins = jnp.broadcast_to(bin_ref[...].astype(F32), (2, LANES))
    classes = jnp.broadcast_to(class_ref[...].astype(F32), (2, LANES))
    for t in range(8):
        rem = [tpl_ref[b, :, pl.ds((64 + t) * LANES, LANES)] for b in range(4)]
        for q in range(4):
            dest = 4 * t + q
            for j in range(2):
                for b in range(4):
                    out_ref[dest, pl.ds(16 * j + 4 * b, 4), :] = tpl_ref[b, :, pl.ds((2 * dest + j) * LANES, LANES)]
            out_ref[dest, pl.ds(32, 4), :] = pick_groups([turned(rem[b], b - q) for b in range(4)])
            out_ref[dest, pl.ds(META, 2), :] = bins
            out_ref[dest, pl.ds(META + 2, 2), :] = classes


def pack_templates(templates, bins, classes):
    whole = lambda shape: pl.BlockSpec(shape, lambda i: (0,) * len(shape))
    return pl.pallas_call(
        pack_templates_kernel,
        grid=(1,),
        in_specs=[whole(templates.shape), whole((1, LANES)), whole((1, LANES))],
        out_specs=whole((32, TPL, LANES)),
        out_shape=jax.ShapeDtypeStruct((32, TPL, LANES), F32),
        compiler_params=params(60),
        cost_estimate=cost(0, 1_300_000),
        name="pack_templates",
    )(templates, bins, classes)


def operands_kernel(tpl_ref, below_ref, above_ref, ctf_ref, sq_ref, y_ref, ce_ref, tf_ref):
    for block in range(4):
        for d in range(16):
            at = lambda rows: (below_ref, tpl_ref, tpl_ref, above_ref)[block][(d, 2 * d, 2 * d + 1, d)[block], rows, :]
            rows = pl.ds(16 * d, 16)
            tf_ref[rows, pl.ds(0, 128)] = at(pl.ds(0, 16))
            tf_ref[rows, pl.ds(128, 128)] = at(pl.ds(16, 16))
            packed = at(pl.ds(32, 4))
            v = [turned(packed, j) for j in range(4)]
            for b in range(4):
                tail = pick_groups([v[(q - b) % 4] for q in (0, 1, 2)] + [jnp.zeros_like(packed)])
                tf_ref[pl.ds(16 * d + 4 * b, 4), pl.ds(256, 128)] = tail
        for c in range(4):
            out = pl.ds(256 * block + 64 * c, 64)
            full = tf_ref[pl.ds(64 * c, 64), :]
            quad = jnp.dot(full * full, sq_ref[...], precision=HIGHEST, preferred_element_type=F32)
            hi, lo = split(full)
            vh, vl = split(-0.5 * quad)
            lane = lax.broadcasted_iota(jnp.int32, (64, LANES), 1)
            last = jnp.where(lane < 112, vh.astype(F32), vl.astype(F32))
            tail = jnp.where(lane < 64, hi[:, 256:].astype(F32), lo[:, 256:].astype(F32))
            y_ref[out, pl.ds(0, 256)] = hi[:, :256]
            y_ref[out, pl.ds(256, 256)] = lo[:, :256]
            y_ref[out, pl.ds(512, 128)] = jnp.where(lane < 96, tail, last).astype(BF)
    ctf = ctf_ref[...]
    hi, mid = split(ctf)
    ce_ref[pl.ds(0, 16), :] = hi
    ce_ref[pl.ds(16, 16), :] = mid
    ce_ref[pl.ds(32, 16), :] = (ctf - hi.astype(F32) - mid.astype(F32)).astype(BF)


def operands(tpl, below, above, ctf_ext, squares):
    vmem = pl.BlockSpec(memory_space=pltpu.VMEM)
    return pl.pallas_call(
        operands_kernel,
        in_specs=[vmem] * 5,
        out_specs=[vmem, vmem],
        out_shape=[jax.ShapeDtypeStruct((1024, 640), BF), jax.ShapeDtypeStruct((48, 384), BF)],
        scratch_shapes=[pltpu.VMEM((256, 384), F32)],
        compiler_params=params(12),
        cost_estimate=cost(600_000_000, 4_000_000),
        name="operands",
    )(tpl, below, above, ctf_ext, squares)


def bins_of(tpl_ref, sources):
    rows = [tpl_ref[s, pl.ds(META, 1), :] for s in sources]
    return jnp.concatenate(rows, axis=1).astype(jnp.int32)


def weigh(buf_ref, step, tpl_ref, ce_ref, x_ref, xh_ref, xl_ref, xr_ref):
    group = lane_group((128, LANES))
    for s in range(4):
        source = 4 * step + s
        classes = tpl_ref[source, pl.ds(META + 2, 1), :].astype(jnp.int32)
        row_class = lax.broadcasted_iota(jnp.int32, (48, 128), 0) % CLASSES
        onehot = jnp.where(row_class == classes, 1.0, 0.0).astype(BF)
        ctf = lax.dot_general(onehot, ce_ref[...], (((0,), (0,)), ((), ())), preferred_element_type=F32)
        rows = pl.ds(256 * (s % 2) + 128 * (s // 2), 128)
        for j in range(2):
            hi, lo = split(ctf[:, 128 * j : 128 * j + 128] * buf_ref[s, pl.ds(128 * j, 128), :])
            xh_ref[source, :, pl.ds(128 * j, 128)] = hi
            xl_ref[source, :, pl.ds(128 * j, 128)] = lo
            x_ref[rows, pl.ds(128 * j, 128)] = hi
            x_ref[rows, pl.ds(256 + 128 * j, 128)] = lo
        packed = buf_ref[s, pl.ds(256, 32), :]
        v = [turned(packed, j) for j in range(4)]
        one = jnp.ones_like(packed)
        rem = jnp.concatenate([pick_groups([v[(q - g) % 4] for q in (0, 1, 2)] + [one]) for g in range(4)], axis=0)
        hi, lo = split(ctf[:, 256:] * rem)
        tail = jnp.where(group == 1, lo.astype(F32), hi.astype(F32)).astype(BF)
        xr_ref[source] = tail
        x_ref[rows, pl.ds(512, 128)] = tail


def score(step, x_ref, tpl_ref, y_ref, out_ref):
    row_bin = lax.broadcasted_iota(jnp.int32, (256, 256), 0) // 4
    for side in range(2):
        pair = (4 * step + side, 4 * step + 2 + side)
        x = x_ref[pl.ds(256 * side, 256), :]
        x = jnp.concatenate([x[:, :256], x], axis=1)
        mine = row_bin == bins_of(tpl_ref, pair)
        y = y_ref[pl.ds(256 * side, 768), :]
        y = jnp.concatenate([y[:, :512], y[:, :256], y[:, 512:]], axis=1)
        all_rows = lax.dot_general(y, x, (((1,), (1,)), ((), ())), preferred_element_type=F32)
        for k in range(3):
            kept = jnp.where(mine, all_rows[256 * k : 256 * k + 256], 0.0)
            total = jnp.sum(kept.reshape(32, 8, 256), axis=0)
            total = total + pltpu.roll(total, 4, 0)
            for half, s in enumerate(pair):
                out_ref[3 * s + k] = total[:4, 128 * half : 128 * half + 128]


def scores_kernel(first_ref, odd_ref, even_ref, tpl_ref, y_ref, ce_ref, xh_ref, xl_ref, xr_ref, out_ref, xa_ref, xb_ref):
    i = pl.program_id(0)
    last = 2 * pl.num_programs(0) - 1
    kept = (xh_ref, xl_ref, xr_ref)

    @pl.when(i == 0)
    def _():
        weigh(first_ref, 0, tpl_ref, ce_ref, xa_ref, *kept)

    weigh(odd_ref, 2 * i + 1, tpl_ref, ce_ref, xb_ref, *kept)
    score(2 * i, xa_ref, tpl_ref, y_ref, out_ref)
    weigh(even_ref, jnp.minimum(2 * i + 2, last), tpl_ref, ce_ref, xa_ref, *kept)
    score(2 * i + 1, xb_ref, tpl_ref, y_ref, out_ref)


def window_scores(buf, tpl, y, ctf):
    n = buf.shape[0]
    blocks = n // 4
    vmem = pl.BlockSpec(memory_space=pltpu.VMEM)
    image = lambda at: pl.BlockSpec((4, IMG, LANES), lambda p: (at(p), 0, 0))
    return pl.pallas_call(
        scores_kernel,
        grid=(blocks // 2,),
        in_specs=[image(lambda p: 0), image(lambda p: 2 * p + 1), image(lambda p: jnp.minimum(2 * p + 2, blocks - 1))] + [vmem] * 3,
        out_specs=[vmem] * 4,
        out_shape=[
            jax.ShapeDtypeStruct((n, 128, 256), BF),
            jax.ShapeDtypeStruct((n, 128, 256), BF),
            jax.ShapeDtypeStruct((n, 128, 128), BF),
            jax.ShapeDtypeStruct((3 * n, 4, 128), F32),
        ],
        scratch_shapes=[pltpu.VMEM((512, 640), BF), pltpu.VMEM((512, 640), BF)],
        compiler_params=params(24),
        cost_estimate=cost(6_000_000_000, 14_000_000),
        name="window_scores",
    )(buf, buf, buf, tpl, y, ctf)


def home_kernel(scores_ref, centre_ref, total_ref, shift_ref, p_ref):
    n = scores_ref.shape[0] // 3
    start = 4 * lax.axis_index("xlo") + 8 * lax.axis_index("z") - 4 - centre_ref[...]
    row = lax.broadcasted_iota(jnp.int32, (4, 128), 0)
    offsets, inside, safe = [], [], []
    for k in range(3):
        scores = scores_ref[k]
        for s in range(1, n):
            scores = scores + scores_ref[3 * s + k]
        offset = row + 4 * k + start
        keep = jnp.abs(offset) <= HALF
        offsets.append(offset.astype(F32))
        inside.append(keep)
        safe.append(jnp.where(keep, scores, 0.0))
    mass = sum(jnp.where(keep, jnp.exp(v), 0.0) for keep, v in zip(inside, safe))
    total = jnp.log(jnp.sum(mass, axis=0, keepdims=True))
    p = [jnp.where(keep, jnp.exp(v - total), 0.0) for keep, v in zip(inside, safe)]
    total_ref[...] = total
    shift_ref[...] = jnp.sum(sum(a * b for a, b in zip(p, offsets)), axis=0, keepdims=True)
    for k in range(3):
        for s in range(n):
            p_ref[3 * s + k] = p[k]


def home(scores, centre):
    vmem = pl.BlockSpec(memory_space=pltpu.VMEM)
    return pl.pallas_call(
        home_kernel,
        in_specs=[vmem, vmem],
        out_specs=[vmem, vmem, vmem],
        out_shape=[
            jax.ShapeDtypeStruct((1, 128), F32),
            jax.ShapeDtypeStruct((1, 128), F32),
            jax.ShapeDtypeStruct(scores.shape, F32),
        ],
        compiler_params=params(4),
        cost_estimate=cost(200_000, 600_000),
        name="home",
    )(scores, centre)


def spread(p8, bins, first_bin, rows):
    n = p8.shape[1]
    row_bin = lax.broadcasted_iota(jnp.int32, (rows, n), 0) // 4 + first_bin
    mine = row_bin == bins
    hi = p8.astype(BF).astype(F32)
    lo = p8 - hi
    wide = lambda v: jnp.broadcast_to(v[None], (rows // 8, 8, n)).reshape(rows, n)
    return [jnp.where(mine, wide(v), 0.0).astype(BF) for v in (hi, lo)]


def sums_kernel(which, group, p_ref, tpl_ref, xh_ref, xl_ref, xr_ref, out_ref):
    step = pl.program_id(0)

    @pl.when(step == 0)
    def _():
        out_ref[...] = jnp.zeros_like(out_ref)

    def add(rows, parts, sources):
        stack = lambda ref: jnp.concatenate([ref[s] for s in sources], axis=0)
        xh, xl, xr = stack(xh_ref), stack(xl_ref), stack(xr_ref)
        high = jnp.concatenate([part[0] for part in parts], axis=0)
        low = jnp.concatenate([part[1] for part in parts], axis=0)
        left = jnp.concatenate([high, low, high], axis=1)
        main = jnp.dot(left, jnp.concatenate([xh, xh, xl], axis=0), preferred_element_type=F32)
        wide = left.shape[1] // 3 * 2
        tail = jnp.dot(left[:, :wide], jnp.concatenate([xr, xr], axis=0), preferred_element_type=F32)
        out_ref[rows, pl.ds(0, 256)] += main
        out_ref[rows, pl.ds(256, 128)] += tail

    def twice(sources, blocks):
        p4 = jnp.concatenate([p_ref[3 * s + k] for s, k in zip(sources, blocks)], axis=1)
        return jnp.concatenate([p4, p4], axis=0)

    if which == "halo":
        for side in range(2):
            mine = [group * step + s for s in range(side, group, 2)]
            p8 = twice(mine, [2 * side] * len(mine))
            add(pl.ds(256 * side, 256), [spread(p8, bins_of(tpl_ref, mine), 0, 256)], mine)
    else:
        mine = [group * step + s for s in range(group)]
        bins = bins_of(tpl_ref, mine)
        parts = [spread(twice(mine, [k + 1, k] * (group // 2)), bins, 0, 256) for k in range(2)]
        add(pl.ds(0, 512), parts, mine)


def sums(which, p, tpl, xh, xl, xr, group=32):
    n = xh.shape[0]
    vmem = pl.BlockSpec(memory_space=pltpu.VMEM)

    def body(*refs):
        sums_kernel(which, group, *refs)

    return pl.pallas_call(
        body,
        grid=(n // group,),
        in_specs=[vmem] * 5,
        out_specs=vmem,
        out_shape=jax.ShapeDtypeStruct((512, 384), F32),
        compiler_params=params(24),
        cost_estimate=cost(4_000_000_000, 6_000_000),
        name="sums_" + which,
    )(p, tpl, xh, xl, xr)


def average_kernel(own_ref, below_ref, above_ref, sq_ref, out_ref):
    for side, other_ref in ((0, below_ref), (1, above_ref)):
        for c in range(4):
            rows = pl.ds(64 * c, 64)
            total = own_ref[pl.ds(256 * side + 64 * c, 64), :] + other_ref[rows, :]
            weight = jnp.dot(total[:, 256:], sq_ref[...], precision=HIGHEST, preferred_element_type=F32)
            tail = total[:, 256:]
            tail = tail + pltpu.roll(tail, 96, 1)
            mean = jnp.concatenate([total[:, :256], tail], axis=1) / (weight + 1.0)
            for d in range(4):
                dest = 2 * (4 * c + d) + side
                rem = []
                for b in range(4):
                    piece = mean[16 * d + 4 * b : 16 * d + 4 * b + 4]
                    out_ref[9 * dest + b] = piece[:, :128]
                    out_ref[9 * dest + 4 + b] = piece[:, 128:256]
                    rem.append(turned(piece[:, 256:], b))
                out_ref[9 * dest + 8] = pick_groups(rem)


def averages(own, below, above, squares, n):
    vmem = pl.BlockSpec(memory_space=pltpu.VMEM)
    return pl.pallas_call(
        average_kernel,
        in_specs=[vmem] * 4,
        out_specs=vmem,
        out_shape=jax.ShapeDtypeStruct((9 * n, 4, LANES), F32),
        compiler_params=params(8),
        cost_estimate=cost(200_000_000, 3_000_000),
        name="averages",
    )(own, below, above, squares)


def unpack_kernel(got_ref, out_ref):
    n = got_ref.shape[0] // 9
    for i in range(n):
        for j in range(2):
            for b in range(4):
                out_ref[b, :, pl.ds(256 * i + 128 * j, 128)] = got_ref[9 * i + 4 * j + b]
    for t in range(n // 4):
        rem = [got_ref[9 * (4 * t + q) + 8] for q in range(4)]
        for b in range(4):
            out_ref[b, :, pl.ds(256 * n + 128 * t, 128)] = pick_groups([turned(rem[q], q - b) for q in range(4)])


def unpack(got, pixels):
    vmem = pl.BlockSpec(memory_space=pltpu.VMEM)
    return pl.pallas_call(
        unpack_kernel,
        in_specs=[vmem],
        out_specs=vmem,
        out_shape=jax.ShapeDtypeStruct((4, 4, pixels), F32),
        compiler_params=params(8),
        cost_estimate=cost(0, 1_200_000),
        name="unpack",
    )(got)


def exchange(value):
    return lax.all_to_all(value, PLANE, split_axis=0, concat_axis=0, tiled=True)


def along_z(value, by):
    size = lax.axis_size("z")
    return lax.ppermute(value, "z", [(i, (i + by) % size) for i in range(size)])


def local(images, prior_bin, prior_center, defocus_class, templates, ctf_table):
    pixels = images.shape[1]
    xlo = lax.axis_index("xlo")
    chunk = lax.axis_index("dir") * 2 + xlo
    ctf_main = lax.dynamic_slice(ctf_table, (0, 256 * chunk), (CLASSES, 256))
    ctf_rem = lax.dynamic_slice(ctf_table, (0, 8192 + 32 * chunk), (CLASSES, 32))
    eye = jnp.eye(CLASSES, dtype=F32)
    ctf_ext = jnp.concatenate([ctf_main, ctf_rem, ctf_rem, ctf_rem, eye, eye], axis=1)
    square = jnp.concatenate([ctf_main, ctf_rem], axis=1)
    square = square * square
    to_class = jnp.pad(jnp.concatenate([square.T, square.T], axis=1), ((0, 96), (96, 0)))
    to_pixel = jnp.pad(square, ((96, 16), (0, 96)))

    tpl = exchange(pack_templates(templates, prior_bin[None], defocus_class[None]))
    n = tpl.shape[0]
    buf = exchange(pack_images(images))
    sides = tpl.reshape(n // 2, 2, TPL, LANES)
    below = along_z(sides[:, 1], 1)
    above = along_z(sides[:, 0], -1)
    y, ctf = operands(tpl, below, above, ctf_ext, to_class)
    xh, xl, xr, partial = window_scores(buf, tpl, y, ctf)
    log_total, mean_shift, p = home(exchange(partial), prior_center[None])
    p = exchange(p)
    edge = sums("halo", p, tpl, xh, xl, xr)
    from_above = along_z(edge[:256], -1)
    from_below = along_z(edge[256:], 1)
    mine = sums("own", p, tpl, xh, xl, xr)
    out = averages(mine, from_below, from_above, to_pixel, n)
    average = unpack(exchange(out), pixels)
    return log_total[0], mean_shift[0], average


def solution(mesh):
    dirs, psis = mesh.devices.shape
    fine = Mesh(mesh.devices.reshape(dirs, psis // 2, 2), ("dir", "z", "xlo"))
    rows = P(("dir", "z", "xlo"))
    grid = P("dir", ("z", "xlo"), None)
    return jax.shard_map(
        local,
        mesh=fine,
        in_specs=(P(("dir", "z", "xlo"), None), rows, rows, rows, grid, P()),
        out_specs=(rows, rows, grid),
        check_vma=False,
    )
```

```python
import jax
import jax.numpy as jnp
from jax import lax
from jax.experimental import pallas as pl
from jax.experimental.pallas import tpu as pltpu
from jax.sharding import Mesh
from jax.sharding import PartitionSpec as P

HALF = 4
LANES = 128
CLASSES = 16
IMG = 288
TPL = 40
META = 36
BF = jnp.bfloat16
F32 = jnp.float32
HIGHEST = lax.Precision.HIGHEST
PLANE = ("dir", "xlo")


def params(mib):
    return pltpu.CompilerParams(vmem_limit_bytes=mib * 1024 * 1024)


def cost(flops, moved):
    return pl.CostEstimate(flops=flops, bytes_accessed=moved, transcendentals=0)


def lane_group(shape):
    return lax.broadcasted_iota(jnp.int32, shape, len(shape) - 1) // 32


def turned(x, groups):
    groups = groups % 4
    return x if groups == 0 else pltpu.roll(x, 32 * groups, x.ndim - 1)


def pick_groups(parts):
    group = lane_group(parts[0].shape)
    out = parts[3]
    for q in (2, 1, 0):
        out = jnp.where(group == q, parts[q], out)
    return out


def split(x):
    hi = x.astype(BF)
    return hi, (x - hi.astype(F32)).astype(BF)


def pack_images_kernel(img_ref, rem_ref, out_ref):
    for q in range(4):
        for j in range(2):
            out_ref[q, pl.ds(j * 128, 128), :] = img_ref[:, pl.ds((2 * q + j) * LANES, LANES)]
        out_ref[q, pl.ds(256, 32), :] = pick_groups([turned(rem_ref[pl.ds(32 * g, 32), :], g - q) for g in range(4)])


def pack_images(images):
    steps = 8
    return pl.pallas_call(
        pack_images_kernel,
        grid=(steps,),
        in_specs=[
            pl.BlockSpec((128, 1024), lambda t: (0, t)),
            pl.BlockSpec((128, LANES), lambda t: (0, 64 + t)),
        ],
        out_specs=pl.BlockSpec((4, IMG, LANES), lambda t: (t, 0, 0)),
        out_shape=jax.ShapeDtypeStruct((4 * steps, IMG, LANES), F32),
        compiler_params=params(60),
        cost_estimate=cost(0, 9_500_000),
        name="pack_images",
    )(images, images)


def pack_templates_kernel(tpl_ref, bin_ref, class_ref, out_ref):
    bins = jnp.broadcast_to(bin_ref[...].astype(F32), (2, LANES))
    classes = jnp.broadcast_to(class_ref[...].astype(F32), (2, LANES))
    for t in range(8):
        rem = [tpl_ref[b, :, pl.ds((64 + t) * LANES, LANES)] for b in range(4)]
        for q in range(4):
            dest = 4 * t + q
            for j in range(2):
                for b in range(4):
                    out_ref[dest, pl.ds(16 * j + 4 * b, 4), :] = tpl_ref[b, :, pl.ds((2 * dest + j) * LANES, LANES)]
            out_ref[dest, pl.ds(32, 4), :] = pick_groups([turned(rem[b], b - q) for b in range(4)])
            out_ref[dest, pl.ds(META, 2), :] = bins
            out_ref[dest, pl.ds(META + 2, 2), :] = classes


def pack_templates(templates, bins, classes):
    whole = lambda shape: pl.BlockSpec(shape, lambda i: (0,) * len(shape))
    return pl.pallas_call(
        pack_templates_kernel,
        grid=(1,),
        in_specs=[whole(templates.shape), whole((1, LANES)), whole((1, LANES))],
        out_specs=whole((32, TPL, LANES)),
        out_shape=jax.ShapeDtypeStruct((32, TPL, LANES), F32),
        compiler_params=params(60),
        cost_estimate=cost(0, 1_300_000),
        name="pack_templates",
    )(templates, bins, classes)


def operands_kernel(tpl_ref, below_ref, above_ref, ctf_ref, sq_ref, y_ref, ce_ref, tf_ref):
    for block in range(4):
        for d in range(16):
            at = lambda rows: (below_ref, tpl_ref, tpl_ref, above_ref)[block][(d, 2 * d, 2 * d + 1, d)[block], rows, :]
            rows = pl.ds(16 * d, 16)
            tf_ref[rows, pl.ds(0, 128)] = at(pl.ds(0, 16))
            tf_ref[rows, pl.ds(128, 128)] = at(pl.ds(16, 16))
            packed = at(pl.ds(32, 4))
            v = [turned(packed, j) for j in range(4)]
            for b in range(4):
                tail = pick_groups([v[(q - b) % 4] for q in (0, 1, 2)] + [jnp.zeros_like(packed)])
                tf_ref[pl.ds(16 * d + 4 * b, 4), pl.ds(256, 128)] = tail
        for c in range(4):
            out = pl.ds(256 * block + 64 * c, 64)
            full = tf_ref[pl.ds(64 * c, 64), :]
            quad = jnp.dot(full * full, sq_ref[...], precision=HIGHEST, preferred_element_type=F32)
            hi, lo = split(full)
            vh, vl = split(-0.5 * quad)
            lane = lax.broadcasted_iota(jnp.int32, (64, LANES), 1)
            last = jnp.where(lane < 112, vh.astype(F32), vl.astype(F32))
            tail = jnp.where(lane < 64, hi[:, 256:].astype(F32), lo[:, 256:].astype(F32))
            y_ref[out, pl.ds(0, 256)] = hi[:, :256]
            y_ref[out, pl.ds(256, 256)] = lo[:, :256]
            y_ref[out, pl.ds(512, 128)] = jnp.where(lane < 96, tail, last).astype(BF)
    ctf = ctf_ref[...]
    hi, mid = split(ctf)
    ce_ref[pl.ds(0, 16), :] = hi
    ce_ref[pl.ds(16, 16), :] = mid
    ce_ref[pl.ds(32, 16), :] = (ctf - hi.astype(F32) - mid.astype(F32)).astype(BF)


def operands(tpl, below, above, ctf_ext, squares):
    vmem = pl.BlockSpec(memory_space=pltpu.VMEM)
    return pl.pallas_call(
        operands_kernel,
        in_specs=[vmem] * 5,
        out_specs=[vmem, vmem],
        out_shape=[jax.ShapeDtypeStruct((1024, 640), BF), jax.ShapeDtypeStruct((48, 384), BF)],
        scratch_shapes=[pltpu.VMEM((256, 384), F32)],
        compiler_params=params(12),
        cost_estimate=cost(600_000_000, 4_000_000),
        name="operands",
    )(tpl, below, above, ctf_ext, squares)


def bins_of(tpl_ref, sources):
    rows = [tpl_ref[s, pl.ds(META, 1), :] for s in sources]
    return jnp.concatenate(rows, axis=1).astype(jnp.int32)


def weigh(buf_ref, step, tpl_ref, ce_ref, x_ref, xh_ref, xl_ref, xr_ref):
    group = lane_group((128, LANES))
    for s in range(4):
        source = 4 * step + s
        classes = tpl_ref[source, pl.ds(META + 2, 1), :].astype(jnp.int32)
        row_class = lax.broadcasted_iota(jnp.int32, (48, 128), 0) % CLASSES
        onehot = jnp.where(row_class == classes, 1.0, 0.0).astype(BF)
        ctf = lax.dot_general(onehot, ce_ref[...], (((0,), (0,)), ((), ())), preferred_element_type=F32)
        rows = pl.ds(256 * (s % 2) + 128 * (s // 2), 128)
        for j in range(2):
            hi, lo = split(ctf[:, 128 * j : 128 * j + 128] * buf_ref[s, pl.ds(128 * j, 128), :])
            xh_ref[source, :, pl.ds(128 * j, 128)] = hi
            xl_ref[source, :, pl.ds(128 * j, 128)] = lo
            x_ref[rows, pl.ds(128 * j, 128)] = hi
            x_ref[rows, pl.ds(256 + 128 * j, 128)] = lo
        packed = buf_ref[s, pl.ds(256, 32), :]
        v = [turned(packed, j) for j in range(4)]
        one = jnp.ones_like(packed)
        rem = jnp.concatenate([pick_groups([v[(q - g) % 4] for q in (0, 1, 2)] + [one]) for g in range(4)], axis=0)
        hi, lo = split(ctf[:, 256:] * rem)
        tail = jnp.where(group == 1, lo.astype(F32), hi.astype(F32)).astype(BF)
        xr_ref[source] = tail
        x_ref[rows, pl.ds(512, 128)] = tail


def score(step, x_ref, tpl_ref, y_ref, out_ref):
    row_bin = lax.broadcasted_iota(jnp.int32, (256, 256), 0) // 4
    for side in range(2):
        pair = (4 * step + side, 4 * step + 2 + side)
        x = x_ref[pl.ds(256 * side, 256), :]
        x = jnp.concatenate([x[:, :256], x], axis=1)
        mine = row_bin == bins_of(tpl_ref, pair)
        y = y_ref[pl.ds(256 * side, 768), :]
        y = jnp.concatenate([y[:, :512], y[:, :256], y[:, 512:]], axis=1)
        all_rows = lax.dot_general(y, x, (((1,), (1,)), ((), ())), preferred_element_type=F32)
        for k in range(3):
            kept = jnp.where(mine, all_rows[256 * k : 256 * k + 256], 0.0)
            total = jnp.sum(kept.reshape(32, 8, 256), axis=0)
            total = total + pltpu.roll(total, 4, 0)
            for half, s in enumerate(pair):
                out_ref[3 * s + k] = total[:4, 128 * half : 128 * half + 128]


def scores_kernel(first_ref, odd_ref, even_ref, tpl_ref, y_ref, ce_ref, xh_ref, xl_ref, xr_ref, out_ref, xa_ref, xb_ref):
    i = pl.program_id(0)
    last = 2 * pl.num_programs(0) - 1
    kept = (xh_ref, xl_ref, xr_ref)

    @pl.when(i == 0)
    def _():
        weigh(first_ref, 0, tpl_ref, ce_ref, xa_ref, *kept)

    weigh(odd_ref, 2 * i + 1, tpl_ref, ce_ref, xb_ref, *kept)
    score(2 * i, xa_ref, tpl_ref, y_ref, out_ref)
    weigh(even_ref, jnp.minimum(2 * i + 2, last), tpl_ref, ce_ref, xa_ref, *kept)
    score(2 * i + 1, xb_ref, tpl_ref, y_ref, out_ref)


def window_scores(buf, tpl, y, ctf):
    n = buf.shape[0]
    blocks = n // 4
    vmem = pl.BlockSpec(memory_space=pltpu.VMEM)
    image = lambda at: pl.BlockSpec((4, IMG, LANES), lambda p: (at(p), 0, 0))
    return pl.pallas_call(
        scores_kernel,
        grid=(blocks // 2,),
        in_specs=[image(lambda p: 0), image(lambda p: 2 * p + 1), image(lambda p: jnp.minimum(2 * p + 2, blocks - 1))] + [vmem] * 3,
        out_specs=[vmem] * 4,
        out_shape=[
            jax.ShapeDtypeStruct((n, 128, 256), BF),
            jax.ShapeDtypeStruct((n, 128, 256), BF),
            jax.ShapeDtypeStruct((n, 128, 128), BF),
            jax.ShapeDtypeStruct((3 * n, 4, 128), F32),
        ],
        scratch_shapes=[pltpu.VMEM((512, 640), BF), pltpu.VMEM((512, 640), BF)],
        compiler_params=params(24),
        cost_estimate=cost(6_000_000_000, 14_000_000),
        name="window_scores",
    )(buf, buf, buf, tpl, y, ctf)


def home_kernel(scores_ref, centre_ref, total_ref, shift_ref, p_ref):
    n = scores_ref.shape[0] // 3
    start = 4 * lax.axis_index("xlo") + 8 * lax.axis_index("z") - 4 - centre_ref[...]
    row = lax.broadcasted_iota(jnp.int32, (4, 128), 0)
    offsets, inside, safe = [], [], []
    for k in range(3):
        scores = scores_ref[k]
        for s in range(1, n):
            scores = scores + scores_ref[3 * s + k]
        offset = row + 4 * k + start
        keep = jnp.abs(offset) <= HALF
        offsets.append(offset.astype(F32))
        inside.append(keep)
        safe.append(jnp.where(keep, scores, 0.0))
    mass = sum(jnp.where(keep, jnp.exp(v), 0.0) for keep, v in zip(inside, safe))
    total = jnp.log(jnp.sum(mass, axis=0, keepdims=True))
    p = [jnp.where(keep, jnp.exp(v - total), 0.0) for keep, v in zip(inside, safe)]
    total_ref[...] = total
    shift_ref[...] = jnp.sum(sum(a * b for a, b in zip(p, offsets)), axis=0, keepdims=True)
    for k in range(3):
        for s in range(n):
            p_ref[3 * s + k] = p[k]


def home(scores, centre):
    vmem = pl.BlockSpec(memory_space=pltpu.VMEM)
    return pl.pallas_call(
        home_kernel,
        in_specs=[vmem, vmem],
        out_specs=[vmem, vmem, vmem],
        out_shape=[
            jax.ShapeDtypeStruct((1, 128), F32),
            jax.ShapeDtypeStruct((1, 128), F32),
            jax.ShapeDtypeStruct(scores.shape, F32),
        ],
        compiler_params=params(4),
        cost_estimate=cost(200_000, 600_000),
        name="home",
    )(scores, centre)


def spread(p8, bins, first_bin, rows):
    n = p8.shape[1]
    row_bin = lax.broadcasted_iota(jnp.int32, (rows, n), 0) // 4 + first_bin
    mine = row_bin == bins
    hi = p8.astype(BF).astype(F32)
    lo = p8 - hi
    wide = lambda v: jnp.broadcast_to(v[None], (rows // 8, 8, n)).reshape(rows, n)
    return [jnp.where(mine, wide(v), 0.0).astype(BF) for v in (hi, lo)]


def pack_tail(tail):
    group = lane_group((256, LANES))
    tail = jnp.where(group == 0, tail + pltpu.roll(tail, 96, 1), tail)
    first, second = tail[:128], pltpu.roll(tail[128:], 64, 1)
    both = pick_groups([first, second, second, first])
    return jnp.concatenate([both[:64], both[64:]], axis=1)


def unpack_tail(ref, rows):
    half = pl.ds(128 * (rows % 2), 128)
    both = ref[pl.ds(256, 64), half]
    both = both if rows < 2 else pltpu.roll(both, 64, 1)
    group = lane_group((64, LANES))
    return jnp.where(jnp.logical_or(group == 0, group == 3), both, 0.0)


def edge_kernel(p_ref, tpl_ref, xh_ref, xl_ref, xr_ref, below_ref, above_ref):
    n = xh_ref.shape[0]
    for side, out_ref in enumerate((below_ref, above_ref)):
        mine = range(side, n, 2)
        stack = lambda ref: jnp.concatenate([ref[s] for s in mine], axis=0)
        xh, xl, xr = stack(xh_ref), stack(xl_ref), stack(xr_ref)
        p4 = jnp.concatenate([p_ref[3 * s + 2 * side] for s in mine], axis=1)
        high, low = spread(jnp.concatenate([p4, p4], axis=0), bins_of(tpl_ref, mine), 0, 256)
        left = jnp.concatenate([high, low, high], axis=1)
        out_ref[pl.ds(0, 256), :] = jnp.dot(left, jnp.concatenate([xh, xh, xl], axis=0), preferred_element_type=F32)
        wide = left.shape[1] // 3 * 2
        tail = jnp.dot(left[:, :wide], jnp.concatenate([xr, xr], axis=0), preferred_element_type=F32)
        out_ref[pl.ds(256, 64), :] = pack_tail(tail)


def edge_sums(p, tpl, xh, xl, xr):
    vmem = pl.BlockSpec(memory_space=pltpu.VMEM)
    return pl.pallas_call(
        edge_kernel,
        in_specs=[vmem] * 5,
        out_specs=[vmem] * 2,
        out_shape=[jax.ShapeDtypeStruct((320, 256), F32)] * 2,
        compiler_params=params(24),
        cost_estimate=cost(3_000_000_000, 6_000_000),
        name="edge_sums",
    )(p, tpl, xh, xl, xr)


def sums_kernel(which, group, p_ref, tpl_ref, xh_ref, xl_ref, xr_ref, out_ref):
    step = pl.program_id(0)

    @pl.when(step == 0)
    def _():
        out_ref[...] = jnp.zeros_like(out_ref)

    def add(rows, parts, sources):
        stack = lambda ref: jnp.concatenate([ref[s] for s in sources], axis=0)
        xh, xl, xr = stack(xh_ref), stack(xl_ref), stack(xr_ref)
        high = jnp.concatenate([part[0] for part in parts], axis=0)
        low = jnp.concatenate([part[1] for part in parts], axis=0)
        left = jnp.concatenate([high, low, high], axis=1)
        main = jnp.dot(left, jnp.concatenate([xh, xh, xl], axis=0), preferred_element_type=F32)
        wide = left.shape[1] // 3 * 2
        tail = jnp.dot(left[:, :wide], jnp.concatenate([xr, xr], axis=0), preferred_element_type=F32)
        out_ref[rows, pl.ds(0, 256)] += main
        out_ref[rows, pl.ds(256, 128)] += tail

    def twice(sources, blocks):
        p4 = jnp.concatenate([p_ref[3 * s + k] for s, k in zip(sources, blocks)], axis=1)
        return jnp.concatenate([p4, p4], axis=0)

    if which == "halo":
        for side in range(2):
            mine = [group * step + s for s in range(side, group, 2)]
            p8 = twice(mine, [2 * side] * len(mine))
            add(pl.ds(256 * side, 256), [spread(p8, bins_of(tpl_ref, mine), 0, 256)], mine)
    else:
        mine = [group * step + s for s in range(group)]
        bins = bins_of(tpl_ref, mine)
        parts = [spread(twice(mine, [k + 1, k] * (group // 2)), bins, 0, 256) for k in range(2)]
        add(pl.ds(0, 512), parts, mine)


def sums(which, p, tpl, xh, xl, xr, group=32):
    n = xh.shape[0]
    vmem = pl.BlockSpec(memory_space=pltpu.VMEM)

    def body(*refs):
        sums_kernel(which, group, *refs)

    return pl.pallas_call(
        body,
        grid=(n // group,),
        in_specs=[vmem] * 5,
        out_specs=vmem,
        out_shape=jax.ShapeDtypeStruct((512, 384), F32),
        compiler_params=params(24),
        cost_estimate=cost(4_000_000_000, 6_000_000),
        name="sums_" + which,
    )(p, tpl, xh, xl, xr)


def average_kernel(own_ref, below_ref, above_ref, square_ref, out_ref, sq_ref):
    sq_ref[...] = jnp.zeros_like(sq_ref)
    sq_ref[pl.ds(96, CLASSES), pl.ds(0, 288)] = square_ref[...]
    for side, other_ref in ((0, below_ref), (1, above_ref)):
        for c in range(4):
            other = jnp.concatenate([other_ref[pl.ds(64 * c, 64), :], unpack_tail(other_ref, c)], axis=1)
            total = own_ref[pl.ds(256 * side + 64 * c, 64), :] + other
            weight = jnp.dot(total[:, 256:], sq_ref[...], precision=HIGHEST, preferred_element_type=F32)
            tail = total[:, 256:]
            tail = tail + pltpu.roll(tail, 96, 1)
            mean = jnp.concatenate([total[:, :256], tail], axis=1) / (weight + 1.0)
            for d in range(4):
                dest = 2 * (4 * c + d) + side
                rem = []
                for b in range(4):
                    piece = mean[16 * d + 4 * b : 16 * d + 4 * b + 4]
                    out_ref[9 * dest + b] = piece[:, :128]
                    out_ref[9 * dest + 4 + b] = piece[:, 128:256]
                    rem.append(turned(piece[:, 256:], b))
                out_ref[9 * dest + 8] = pick_groups(rem)


def averages(own, below, above, squares, n):
    vmem = pl.BlockSpec(memory_space=pltpu.VMEM)
    return pl.pallas_call(
        average_kernel,
        in_specs=[vmem] * 4,
        out_specs=vmem,
        out_shape=jax.ShapeDtypeStruct((9 * n, 4, LANES), F32),
        scratch_shapes=[pltpu.VMEM((128, 384), F32)],
        compiler_params=params(8),
        cost_estimate=cost(200_000_000, 3_000_000),
        name="averages",
    )(own, below, above, squares)


def unpack_kernel(got_ref, out_ref):
    n = got_ref.shape[0] // 9
    for i in range(n):
        for j in range(2):
            for b in range(4):
                out_ref[b, :, pl.ds(256 * i + 128 * j, 128)] = got_ref[9 * i + 4 * j + b]
    for t in range(n // 4):
        rem = [got_ref[9 * (4 * t + q) + 8] for q in range(4)]
        for b in range(4):
            out_ref[b, :, pl.ds(256 * n + 128 * t, 128)] = pick_groups([turned(rem[q], q - b) for q in range(4)])


def unpack(got, pixels):
    vmem = pl.BlockSpec(memory_space=pltpu.VMEM)
    return pl.pallas_call(
        unpack_kernel,
        in_specs=[vmem],
        out_specs=vmem,
        out_shape=jax.ShapeDtypeStruct((4, 4, pixels), F32),
        compiler_params=params(8),
        cost_estimate=cost(0, 1_200_000),
        name="unpack",
    )(got)


def exchange(value):
    return lax.all_to_all(value, PLANE, split_axis=0, concat_axis=0, tiled=True)


def along_z(value, by):
    size = lax.axis_size("z")
    return lax.ppermute(value, "z", [(i, (i + by) % size) for i in range(size)])


def local(images, prior_bin, prior_center, defocus_class, templates, ctf_table):
    pixels = images.shape[1]
    xlo = lax.axis_index("xlo")
    chunk = lax.axis_index("dir") * 2 + xlo
    ctf_main = lax.dynamic_slice(ctf_table, (0, 256 * chunk), (CLASSES, 256))
    ctf_rem = lax.dynamic_slice(ctf_table, (0, 8192 + 32 * chunk), (CLASSES, 32))
    eye = jnp.eye(CLASSES, dtype=F32)
    ctf_ext = jnp.concatenate([ctf_main, ctf_rem, ctf_rem, ctf_rem, eye, eye], axis=1)
    square = jnp.concatenate([ctf_main, ctf_rem], axis=1)
    square = square * square
    to_class = jnp.pad(jnp.concatenate([square.T, square.T], axis=1), ((0, 96), (96, 0)))

    tpl = exchange(pack_templates(templates, prior_bin[None], defocus_class[None]))
    n = tpl.shape[0]
    buf = exchange(pack_images(images))
    sides = tpl.reshape(n // 2, 2, TPL, LANES)
    below = along_z(sides[:, 1], 1)
    above = along_z(sides[:, 0], -1)
    y, ctf = operands(tpl, below, above, ctf_ext, to_class)
    xh, xl, xr, partial = window_scores(buf, tpl, y, ctf)
    log_total, mean_shift, p = home(exchange(partial), prior_center[None])
    p = exchange(p)
    down, up = edge_sums(p, tpl, xh, xl, xr)
    from_above = along_z(down, -1)
    from_below = along_z(up, 1)
    mine = sums("own", p, tpl, xh, xl, xr)
    out = averages(mine, from_below, from_above, square, n)
    average = unpack(exchange(out), pixels)
    return log_total[0], mean_shift[0], average


def solution(mesh):
    dirs, psis = mesh.devices.shape
    fine = Mesh(mesh.devices.reshape(dirs, psis // 2, 2), ("dir", "z", "xlo"))
    rows = P(("dir", "z", "xlo"))
    grid = P("dir", ("z", "xlo"), None)
    return jax.shard_map(
        local,
        mesh=fine,
        in_specs=(P(("dir", "z", "xlo"), None), rows, rows, rows, grid, P()),
        out_specs=(rows, rows, grid),
        check_vma=False,
    )
```
